256 devices in a mesh: ctx: 64 (over y, z, core), head: 4 (over x).
Axes of the slice: x: 4, y: 4, z: 8, core: 2. Of those that a mesh axis runs over, the one named last changes fastest.
Arguments:
- queries: bfloat16 [65536, 4096], P('ctx', 'head'), may hold values from -6.4 to 6.4
- keys: bfloat16 [65536, 4096], P('ctx', 'head'), may hold values from -0.62 to 0.62
- values: bfloat16 [65536, 4096], P('ctx', 'head'), may hold values from -7.6 to 7.6
- log_decay: float32 [32, 65536], P('head', 'ctx'), may hold values from -1.6 to 0, as said below
- gain: float32 [4096], P('head'), may hold values from 0.1 to 1.9
Outputs:
- shift: float32 [4096], P('head')
- covariance: float32 [4096, 2048], P(('head', 'ctx'))
The draws below stay inside these ranges and needn't reach their ends.
Inputs may be any that keep to these rules, and one draw needn't show every extreme that they name: log_decay is negative everywhere.
All inputs are finite; a program needn't handle non-finite values.
Results may differ from the reference program's by a relative error of at most 0.0045.
The reference program's roundings to bfloat16 on the way (of `weights`, `attended` and `centered`) count: a program that leaves them out, or rounds other values in their place, can miss the bound.
Values may be sent and summed in bfloat16 or wider, within the bound.
A program may use at most 128 MiB of HBM per device.

```python
import jax
import jax.numpy as jnp
from jax import lax

HEAD_DIM = 128
HEADS = 32
SPAN = 256
TOK_DEV = 1024
TOKENS = 65536
CH = 4096
CH_DEV = 1024
N_CTX = 64


def head_signs(key):
    coin_flips = jax.random.bernoulli(jax.random.fold_in(key, 4), 0.5, (CH,))
    return jnp.where(coin_flips, 1.0, -1.0).astype(jnp.float32)


def draw_queries(key, part):
    sign_vector = head_signs(key)
    jitter = jnp.clip(jax.random.normal(jax.random.fold_in(key, 1), (TOKENS, CH), jnp.float32), -6.0, 6.0)
    return (jitter + 0.3 * sign_vector[None, :]).astype(jnp.bfloat16)


def draw_keys(key, part):
    sign_vector = head_signs(key)
    jitter = jnp.clip(jax.random.normal(jax.random.fold_in(key, 2), (TOKENS, CH), jnp.float32), -6.0, 6.0)
    offset = 0.13 * TOKENS ** (-0.5)
    return (0.1 * jitter + offset * sign_vector[None, :]).astype(jnp.bfloat16)


def draw_values(key, part):
    jitter = jnp.clip(jax.random.normal(jax.random.fold_in(key, 3), (TOKENS, CH), jnp.float32), -6.0, 6.0)
    magnitude = jnp.exp(jax.random.uniform(jax.random.fold_in(key, 5), (CH,), jnp.float32, jnp.log(0.25), 0.0))
    coin_flips = jax.random.bernoulli(jax.random.fold_in(key, 6), 0.5, (CH,))
    value_signs = jnp.where(coin_flips, 1.0, -1.0).astype(jnp.float32)
    shard_count = TOKENS // TOK_DEV
    drift = jax.random.uniform(jax.random.fold_in(key, 7), (shard_count, CH), jnp.float32, 0.5, 1.5)
    shard_drift = jnp.repeat(drift, TOK_DEV, axis=0)
    offset = (magnitude * value_signs)[None, :] * shard_drift
    return (jitter + offset).astype(jnp.bfloat16)


def draw_log_decay(key, part):
    keys = jax.random.split(key, 6)
    fast_share = 0.5
    picks = jax.random.uniform(keys[0], (HEADS, 1), jnp.float32)
    fast_rate = jnp.exp(jax.random.uniform(keys[1], (HEADS, 1), jnp.float32, jnp.log(1.0 / 50.0), jnp.log(1.0 / 30.0)))
    slow_rate = jnp.exp(jax.random.uniform(keys[2], (HEADS, 1), jnp.float32, jnp.log(0.05), jnp.log(0.8))) / TOKENS
    decay_rate = jnp.where(picks < fast_share, fast_rate, slow_rate)
    coarse_estimate = jax.random.uniform(keys[3], (HEADS, TOKENS), jnp.float32, 0.5, 1.5)
    outlier_spots = jax.random.randint(keys[4], (3,), 0, TOKENS)
    dimension_sizes = jax.random.uniform(keys[5], (3,), jnp.float32, 0.22, 0.5)
    token_position = jnp.arange(TOKENS)
    spike_amount = jnp.sum(jnp.where(token_position[None, :] == outlier_spots[:, None], dimension_sizes[:, None], 0.0), axis=0)
    return (-(decay_rate * coarse_estimate + spike_amount[None, :])).astype(jnp.float32)


def setup_inputs(seed: int = 0) -> dict:
    splits = jax.random.split(jax.random.key(seed), 6)
    queries = draw_queries(jax.random.fold_in(splits[5], 71), 0)
    keys = draw_keys(jax.random.fold_in(splits[5], 71), 0)
    values = draw_values(jax.random.fold_in(splits[5], 71), 0)
    log_decay = draw_log_decay(jax.random.fold_in(splits[5], 71), 0)
    gain = jnp.clip(1.0 + 0.18 * jax.random.normal(splits[4], (CH,), jnp.float32), 0.1, 1.9)
    return dict(queries=queries, keys=keys, values=values, log_decay=log_decay, gain=gain)


def block_step(state, inputs):
    query, key, value, decay = inputs
    cumul = jnp.cumsum(decay, axis=1)
    scores = jnp.einsum('thd,shd->hts', query.astype(jnp.float32), key.astype(jnp.float32))
    length = query.shape[0]
    later = jnp.arange(length)[:, None] >= jnp.arange(length)[None, :]
    diff = cumul[:, :, None] - cumul[:, None, :]
    factor = jnp.where(later[None], jnp.exp(jnp.where(later[None], diff, 0.0)), 0.0)
    weights = (scores * factor).astype(jnp.bfloat16)
    inner = jnp.einsum('hts,shd->thd', weights.astype(jnp.float32), value.astype(jnp.float32))
    scaled_q = query.astype(jnp.float32) * jnp.exp(cumul).T[:, :, None]
    outer = jnp.einsum('thd,hde->the', scaled_q, state, precision=lax.Precision.HIGHEST)
    scaled_k = key.astype(jnp.float32) * jnp.exp(cumul[:, -1:] - cumul).T[:, :, None]
    update = jnp.einsum('shd,she->hde', scaled_k, value.astype(jnp.float32), precision=lax.Precision.HIGHEST)
    new_state = jnp.exp(cumul[:, -1])[:, None, None] * state + update
    return (new_state, inner + outer)

def reference(queries, keys, values, log_decay, gain):
    blocks = TOKENS // SPAN
    query = queries.reshape(blocks, SPAN, HEADS, HEAD_DIM)
    key = keys.reshape(blocks, SPAN, HEADS, HEAD_DIM)
    value = values.reshape(blocks, SPAN, HEADS, HEAD_DIM)
    decay = log_decay.reshape(HEADS, blocks, SPAN).transpose(1, 0, 2)
    start = jnp.zeros((HEADS, HEAD_DIM, HEAD_DIM), jnp.float32)
    _, raw = lax.scan(block_step, start, (query, key, value, decay))
    raw = raw.reshape(TOKENS, HEADS, HEAD_DIM)
    scale = jnp.sqrt(lax.optimization_barrier(jnp.mean(raw * raw, axis=-1, keepdims=True)) + 1e-06)
    attended = (raw / scale * gain.reshape(HEADS, HEAD_DIM)).reshape(TOKENS, CH).astype(jnp.bfloat16)
    wide = attended.astype(jnp.float32)
    shift = (lax.optimization_barrier(jnp.max(wide, axis=0)) + lax.optimization_barrier(jnp.min(wide, axis=0))) / 2.0
    shards = attended.reshape(N_CTX, TOK_DEV, CH)
    width = 2 * CH_DEV
    groups = CH // width

    def add_shard(total, shard):
        means = lax.optimization_barrier(jnp.mean(shard.astype(jnp.float32), axis=0))
        centered = (shard.astype(jnp.float32) - means).astype(jnp.bfloat16)
        parts = []
        for group in range(groups):
            piece = centered[:, group * width:(group + 1) * width]
            parts.append(jnp.dot(piece.T, piece, preferred_element_type=jnp.float32))
        return (total + jnp.stack(parts), means)
    zero = jnp.zeros((groups, width, width), jnp.float32)
    gram, shard_means = lax.scan(add_shard, zero, shards)
    channel_spread = shard_means - lax.optimization_barrier(jnp.mean(shard_means, axis=0))
    rows = []
    for group in range(groups):
        piece = channel_spread[:, group * width:(group + 1) * width]
        fix = TOK_DEV * jnp.dot(piece.T, piece, precision=lax.Precision.HIGHEST)
        rows.append((gram[group] + fix) / TOKENS)
    return (shift, jnp.concatenate(rows, axis=0))
```

```python
import functools

import jax
import jax.numpy as jnp
from jax import lax
from jax.experimental import pallas as pl
from jax.experimental.pallas import tpu as pltpu
from jax.sharding import PartitionSpec as P

D = 128
SPAN = 256
NZ = 8
NY = 4
F32 = jnp.float32
BF16 = jnp.bfloat16
MESH = pl.DeviceIdType.MESH
TOK = (((0,), (0,)), ((), ()))
LAST = (((1,), (1,)), ((), ()))


def place():
    me = lax.axis_index("ctx")
    core = lax.rem(me, 2)
    z = lax.rem(me // 2, NZ)
    y = me // (2 * NZ)
    return y, z, core


def at(y, z, core):
    return {"ctx": (y * NZ + z) * 2 + core}


def greet(peers):
    barrier = pltpu.get_barrier_semaphore()
    for peer in peers:
        pl.semaphore_signal(barrier, inc=1, device_id=peer, device_id_type=MESH)
    return lambda: pl.semaphore_wait(barrier, len(peers))


def send(src, dst, ssem, rsem, peer):
    copy = pltpu.make_async_remote_copy(
        src_ref=src, dst_ref=dst, send_sem=ssem, recv_sem=rsem, device_id=peer, device_id_type=MESH
    )
    copy.start()
    return copy


def arrived(src, dst, ssem, rsem, peer):
    pltpu.make_async_remote_copy(
        src_ref=src, dst_ref=dst, send_sem=ssem, recv_sem=rsem, device_id=peer, device_id_type=MESH
    ).wait_recv()


def plane_peers(y, z, core):
    peers = [at(y, z, 1 - core)]
    peers += [at(y, lax.rem(z + i, NZ), core) for i in range(1, NZ)]
    peers += [at(lax.rem(y + i, NY), z, core) for i in range(1, NY)]
    return peers


def expand(piece):
    return jnp.concatenate(
        [jnp.broadcast_to(piece[64 + i : 65 + i], (16, D)) for i in range(4)], axis=0
    )


def join(first, second):
    return expand(second) * first[:64] + second[:64], first[64:] * second[64:]


def attend_kernel(
    q_ref, k_ref, v_ref, ld_ref, gain_ref, c_ref, st_ref,
    cum, col, inner, upd, part, other, chip, zin, pre, yin, back, chipin, give, sin,
    s_core, r_core, s_z, r_z, s_y, r_y, s_zb, r_zb, s_cb, r_cb,
):
    y, z, core = place()
    ready = greet(plane_peers(y, z, core))
    mate = at(y, z, 1 - core)

    total = ld_ref[...]
    lane = lax.rem(lax.broadcasted_iota(jnp.int32, total.shape, 1), SPAN)
    step = 1
    while step < SPAN:
        total = total + jnp.where(lane >= step, pltpu.roll(total, step, 1), 0.0)
        step *= 2
    cum[...] = total
    turned = jnp.transpose(total)
    for head in range(8):
        col[head] = jnp.broadcast_to(turned[:, head : head + 1], (4 * SPAN, D))
    part[...] = jnp.zeros_like(part)

    def lanes(head):
        return pl.ds(pl.multiple_of(head * D, D), D)

    def update(head):
        ending = jnp.zeros((D, D), F32)
        decay = jnp.zeros((1, D), F32)
        for b in range(4):
            rows = pl.ds(b * SPAN, SPAN)
            last = col[head, pl.ds(b * SPAN + SPAN - 1, 1), :]
            scaled = v_ref[rows, lanes(head)].astype(F32) * jnp.exp(last - col[head, rows, :])
            high = scaled.astype(BF16)
            low = (scaled - high.astype(F32)).astype(BF16)
            both = lax.dot_general(
                k_ref[rows, lanes(head)],
                jnp.concatenate([high, low], axis=1),
                TOK,
                preferred_element_type=F32,
            )
            new = both[:, :D] + both[:, D:]
            upd[head, b] = new
            ending = jnp.exp(last) * ending + new
            decay = decay + last
        half, local = head // 4, lax.rem(head, 4)
        for owner in range(NZ):
            part[half, owner, pl.ds(pl.multiple_of(local * 16, 16), 16), :] = ending[
                owner * 16 : owner * 16 + 16
            ]
            part[half, owner, pl.ds(64 + local, 1), :] = jnp.exp(decay)

    later = lax.broadcasted_iota(jnp.int32, (SPAN, SPAN), 0) >= lax.broadcasted_iota(
        jnp.int32, (SPAN, SPAN), 1
    )

    def within(head):
        for b in range(4):
            rows = pl.ds(b * SPAN, SPAN)
            value = v_ref[rows, lanes(head)]
            scores = lax.dot_general(
                q_ref[rows, lanes(head)], k_ref[rows, lanes(head)], LAST, preferred_element_type=F32
            )
            mine = col[head, rows, :]
            diff = jnp.concatenate([mine, mine], axis=1) - cum[pl.ds(head, 1), rows]
            weights = jnp.where(later, scores * jnp.exp(jnp.minimum(diff, 0.0)), 0.0)
            inner[head, rows, :] = jnp.dot(weights.astype(BF16), value, preferred_element_type=F32)

    def loop(lo, hi, work, shift=0):
        def turn(i, carry):
            work(lax.rem(i + shift, 8))
            return carry

        lax.fori_loop(lo, hi, turn, 0)

    loop(0, 4, update, 4 * (1 - core))
    ready()
    out = [send(part.at[1 - core], other, s_core, r_core, mate)]
    loop(4, 8, update, 4 * (1 - core))
    loop(0, 1, within)
    out[0].wait_recv()

    def combine(owner, carry):
        mine, theirs = part[core, owner], other[owner]
        first = jnp.where(core == 0, mine, theirs)
        second = jnp.where(core == 0, theirs, mine)
        state, decay = join(first, second)
        chip[owner, :64, :] = state
        chip[owner, 64:, :] = decay
        return carry

    lax.fori_loop(0, NZ, combine, 0)
    for i in range(1, NZ):
        to = lax.rem(z + i, NZ)
        out.append(send(chip.at[to], zin.at[z], s_z.at[i], r_z.at[z], at(y, to, core)))
    zin[z] = chip[z]
    loop(1, 4, within)
    for i in range(1, NZ):
        frm = lax.rem(z + i, NZ)
        arrived(chip.at[frm], zin.at[frm], s_z.at[i], r_z.at[frm], at(y, frm, core))
    state, decay = jnp.zeros((64, D), F32), jnp.ones((8, D), F32)
    for j in range(NZ):
        pre[j, :64, :] = state
        pre[j, 64:, :] = decay
        state, decay = join(jnp.concatenate([state, decay], axis=0), zin[j])
    yin[y, :64, :] = state
    yin[y, 64:, :] = decay
    for i in range(1, NY):
        to = lax.rem(y + i, NY)
        out.append(send(yin.at[y], yin.at[y], s_y.at[i], r_y.at[y], at(to, z, core)))
    loop(4, 5, within)
    for i in range(1, NY):
        frm = lax.rem(y + i, NY)
        arrived(yin.at[frm], yin.at[frm], s_y.at[i], r_y.at[frm], at(frm, z, core))
    row = jnp.zeros((64, D), F32)
    for j in range(NY):
        piece = yin[j]
        row = jnp.where(j < y, expand(piece) * row + piece[:64], row)
    for j in range(NZ):
        piece = pre[j]
        back[j] = expand(piece) * row + piece[:64]
    for i in range(1, NZ):
        to = lax.rem(z + i, NZ)
        out.append(send(back.at[to], chipin.at[z], s_zb.at[i], r_zb.at[z], at(y, to, core)))
    chipin[z] = back[z]
    loop(5, 8, within)
    for i in range(1, NZ):
        frm = lax.rem(z + i, NZ)
        arrived(back.at[frm], chipin.at[frm], s_zb.at[i], r_zb.at[frm], at(y, frm, core))

    def split(owner, carry):
        lead = jnp.where(core == 0, part[core, owner], other[owner])
        early = chipin[owner]
        late = expand(lead) * early + lead[:64]
        give[owner] = jnp.where(core == 0, late, early)
        sin[core, owner] = jnp.where(core == 0, early, late)
        return carry

    lax.fori_loop(0, NZ, split, 0)
    out.append(send(give, sin.at[core], s_cb, r_cb, mate))

    def finish(head):
        half, local = head // 4, lax.rem(head, 4)
        state = jnp.concatenate(
            [sin[half, owner, pl.ds(pl.multiple_of(local * 16, 16), 16), :] for owner in range(NZ)],
            axis=0,
        )
        gain = gain_ref[pl.ds(head, 1), :]
        mean = jnp.zeros((1, D), F32)
        top = bottom = None
        made = []
        for b in range(4):
            rows = pl.ds(b * SPAN, SPAN)
            high = state.astype(BF16)
            low = (state - high.astype(F32)).astype(BF16)
            both = jnp.dot(
                q_ref[rows, lanes(head)],
                jnp.concatenate([high, low], axis=1),
                preferred_element_type=F32,
            )
            raw = inner[head, rows, :] + jnp.exp(col[head, rows, :]) * (both[:, :D] + both[:, D:])
            scale = jnp.sqrt(jnp.mean(raw * raw, axis=1, keepdims=True) + 1e-06)
            done = (raw / scale * gain).astype(BF16).astype(F32)
            mean = mean + jnp.sum(done, axis=0, keepdims=True)
            high_b = jnp.max(done, axis=0, keepdims=True)
            low_b = jnp.min(done, axis=0, keepdims=True)
            top = high_b if top is None else jnp.maximum(top, high_b)
            bottom = low_b if bottom is None else jnp.minimum(bottom, low_b)
            made.append(done)
            inner[head, rows, :] = done
            if b < 3:
                last = col[head, pl.ds(b * SPAN + SPAN - 1, 1), :]
                state = jnp.exp(last) * state + upd[head, b]
        mean = mean / (4 * SPAN)
        for b in range(4):
            rows = pl.ds(b * SPAN, SPAN)
            c_ref[rows, lanes(head)] = (inner[head, rows, :] - mean).astype(BF16)
        st_ref[pl.ds(head, 1), :] = mean
        st_ref[pl.ds(8 + head, 1), :] = top
        st_ref[pl.ds(16 + head, 1), :] = bottom

    loop(0, 4, finish, 4 * core)
    out[-1].wait_recv()
    loop(4, 8, finish, 4 * core)
    for copy in out:
        copy.wait_send()


def attend(q, k, v, log_decay, gain):
    count, width = q.shape
    vm = pl.BlockSpec(memory_space=pltpu.VMEM)
    dma = pltpu.SemaphoreType.DMA
    return pl.pallas_call(
        attend_kernel,
        out_shape=(
            jax.ShapeDtypeStruct((count, width), BF16),
            jax.ShapeDtypeStruct((24, D), F32),
        ),
        in_specs=[vm] * 5,
        out_specs=(vm, vm),
        scratch_shapes=[
            pltpu.VMEM((8, 1024), F32),
            pltpu.VMEM((8, 1024, D), F32),
            pltpu.VMEM((8, 1024, D), F32),
            pltpu.VMEM((8, 4, D, D), F32),
            pltpu.VMEM((2, NZ, 72, D), F32),
            pltpu.VMEM((NZ, 72, D), F32),
            pltpu.VMEM((NZ, 72, D), F32),
            pltpu.VMEM((NZ, 72, D), F32),
            pltpu.VMEM((NZ, 72, D), F32),
            pltpu.VMEM((NY, 72, D), F32),
            pltpu.VMEM((NZ, 64, D), F32),
            pltpu.VMEM((NZ, 64, D), F32),
            pltpu.VMEM((NZ, 64, D), F32),
            pltpu.VMEM((2, NZ, 64, D), F32),
            dma, dma, dma((NZ,)), dma((NZ,)), dma((NY,)), dma((NY,)), dma((NZ,)), dma((NZ,)), dma, dma,
        ],
        compiler_params=pltpu.CompilerParams(
            collective_id=0, has_side_effects=True, vmem_limit_bytes=60 * 1024 * 1024
        ),
        name="attend",
    )(q, k, v, log_decay, gain.reshape(8, D))


def gram_kernel(
    c_ref, st_ref, shift_ref, cov_ref,
    theirs, full, grams, mates, sums, ylow, yhigh, ylast, yfirst, ynext, yprev, zsend, zin, strip, hop,
    st1, stsum, stz, sty, off, offin,
    s_x, r_x, s_c, r_c, s_y1, r_y1, s_y2, r_y2, s_z, r_z, s_h, r_h, s_s1, r_s1, s_sz, r_sz, s_sy, r_sy, s_o, r_o,
):
    y, z, core = place()
    parity = lax.rem(lax.axis_index("head"), 2)
    pair = {"head": lax.axis_index("head") + 1 - 2 * parity}
    mate = at(y, z, 1 - core)
    north, south = lax.rem(y + 1, NY), lax.rem(y + NY - 1, NY)
    far = lax.rem(y + 2, NY)
    ready = greet(plane_peers(y, z, core) + [pair])
    ready()
    out = []

    def keep(copy):
        out.append(copy)
        return copy

    other_half = pl.ds(pl.multiple_of((1 - parity) * 512, 512), 512)
    half = pl.ds(pl.multiple_of(parity * 512, 512), 512)
    swap = keep(send(c_ref.at[other_half], theirs, s_x, r_x, pair))
    first = keep(send(st_ref, st1, s_s1, r_s1, mate))

    def diagonal(i):
        full[pl.ds(i * 256, 256), :] = lax.dot_general(
            c_ref[:, i * 256 : i * 256 + 256], c_ref[...], TOK, preferred_element_type=F32
        )

    def merge(a, b):
        return jnp.concatenate(
            [a[:8] + b[:8], jnp.maximum(a[8:16], b[8:16]), jnp.minimum(a[16:], b[16:])], axis=0
        )

    diagonal(0)
    first.wait_recv()
    stz[z] = merge(st_ref[...], st1[...])
    for i in range(1, NZ):
        to = lax.rem(z + i, NZ)
        keep(send(stz.at[z], stz.at[z], s_sz.at[i], r_sz.at[z], at(y, to, core)))
    diagonal(1)
    diagonal(2)
    for i in range(1, NZ):
        frm = lax.rem(z + i, NZ)
        arrived(stz.at[frm], stz.at[frm], s_sz.at[i], r_sz.at[frm], at(y, frm, core))
    sty[y] = functools.reduce(merge, [stz[j] for j in range(NZ)])
    for i in range(1, NY):
        to = lax.rem(y + i, NY)
        keep(send(sty.at[y], sty.at[y], s_sy.at[i], r_sy.at[y], at(to, z, core)))
    diagonal(3)
    for i in range(1, NY):
        frm = lax.rem(y + i, NY)
        arrived(sty.at[frm], sty.at[frm], s_sy.at[i], r_sy.at[frm], at(frm, z, core))
    every = functools.reduce(merge, [sty[j] for j in range(NY)])
    shift_ref[...] = (every[8:16] + every[16:]) / 2.0
    off[...] = st_ref[:8, :] - every[:8] / 64.0
    offset = keep(send(off, offin, s_o, r_o, pair))

    def spread(tall, wide, weight, i):
        column = jnp.transpose(tall)
        rows = [
            jnp.concatenate(
                [
                    weight * jnp.broadcast_to(column[:, h : h + 1], (D, D)) * wide[j : j + 1, :]
                    for j in range(8)
                ],
                axis=1,
            )
            for h in (2 * i, 2 * i + 1)
        ]
        return jnp.concatenate(rows, axis=0)

    def store(seg, i, value):
        grams[seg, pl.ds(8 * i, 8)] = value.astype(BF16).reshape(8, 2, 16, 1024)

    mine = off[...]
    for i in range(4):
        store(0, i, full[pl.ds(i * 256, 256), :] + spread(mine, mine, 1024.0, i))

    def to_mate(seg):
        return keep(send(grams.at[seg, :, 1 - core], mates.at[seg], s_c.at[seg], r_c.at[seg], mate))

    def add_mate(seg, copy):
        copy.wait_recv()

        def turn(i, carry):
            got = grams[seg, i, core].astype(F32) + mates[seg, i].astype(F32)
            sums[seg, i // NZ, lax.rem(i, NZ)] = got.astype(BF16)
            return carry

        lax.fori_loop(0, NZ * NY, turn, 0)
        up = keep(
            send(sums.at[seg, far, :, :, pl.ds(0, 512)], ylow.at[seg], s_y1.at[seg, 0], r_y1.at[seg, 0], at(north, z, core))
        )
        down = keep(
            send(sums.at[seg, far, :, :, pl.ds(512, 512)], yhigh.at[seg], s_y1.at[seg, 1], r_y1.at[seg, 1], at(south, z, core))
        )
        return up, down

    def pass_on(seg, copies):
        copies[0].wait_recv()
        copies[1].wait_recv()

        def turn(i, carry):
            a, b = sums[seg, north, i].astype(F32), sums[seg, south, i].astype(F32)
            low, high = ylow[seg, i].astype(F32), yhigh[seg, i].astype(F32)
            ynext[seg, i] = jnp.concatenate([a[:, :512] + low, a[:, 512:]], axis=1).astype(BF16)
            yprev[seg, i] = jnp.concatenate([b[:, :512], b[:, 512:] + high], axis=1).astype(BF16)
            return carry

        lax.fori_loop(0, NZ, turn, 0)
        up = keep(send(ynext.at[seg], yfirst.at[seg], s_y2.at[seg, 0], r_y2.at[seg, 0], at(north, z, core)))
        down = keep(send(yprev.at[seg], ylast.at[seg], s_y2.at[seg, 1], r_y2.at[seg, 1], at(south, z, core)))
        return up, down

    def to_z(seg, copies):
        copies[0].wait_recv()
        copies[1].wait_recv()

        def turn(i, carry):
            got = sums[seg, y, i].astype(F32) + yfirst[seg, i].astype(F32) + ylast[seg, i].astype(F32)
            zsend[seg, i] = got.astype(BF16)
            return carry

        lax.fori_loop(0, NZ, turn, 0)
        for i in range(1, NZ):
            to = lax.rem(z + i, NZ)
            keep(
                send(zsend.at[seg, to], zin.at[seg, z], s_z.at[seg, i], r_z.at[seg, z], at(y, to, core))
            )
        zin[seg, z] = zsend[seg, z]

    def from_z(seg):
        for i in range(1, NZ):
            frm = lax.rem(z + i, NZ)
            arrived(
                zsend.at[seg, frm], zin.at[seg, frm], s_z.at[seg, i], r_z.at[seg, frm], at(y, frm, core)
            )
        got = zin[seg, 0].astype(F32)
        for j in range(1, NZ):
            got = got + zin[seg, j].astype(F32)
        return got

    core0 = to_mate(0)
    ph1 = add_mate(0, core0)
    ph2 = pass_on(0, ph1)
    offset.wait_recv()
    swap.wait_recv()
    pairs = offin[...]
    for i in range(4):
        value = lax.dot_general(
            theirs[:, i * 256 : i * 256 + 256], c_ref[half, :], TOK, preferred_element_type=F32
        )
        store(1, i, value + spread(pairs, mine, 512.0, i))
    core1 = to_mate(1)
    for i in range(4):
        value = lax.dot_general(
            c_ref[half, i * 256 : i * 256 + 256], theirs[...], TOK, preferred_element_type=F32
        )
        store(2, i, value + spread(mine, pairs, 512.0, i))
    core2 = to_mate(2)
    to_z(0, ph2)
    ph1a = add_mate(1, core1)
    ph1b = add_mate(2, core2)
    ph2a = pass_on(1, ph1a)
    diag = from_z(0)
    ph2b = pass_on(2, ph1b)
    to_z(1, ph2a)
    to_z(2, ph2b)
    strip[...] = from_z(1)
    final = keep(send(strip, hop, s_h, r_h, pair))
    cross = from_z(2)
    final.wait_recv()
    cross = (cross + hop[...]) / 65536.0
    diag = diag / 65536.0
    cov_ref[:, :1024] = jnp.where(parity == 0, diag, cross)
    cov_ref[:, 1024:] = jnp.where(parity == 0, cross, diag)
    for copy in out:
        copy.wait_send()


def gram(centered, stats):
    vm = pl.BlockSpec(memory_space=pltpu.VMEM)
    dma = pltpu.SemaphoreType.DMA
    return pl.pallas_call(
        gram_kernel,
        out_shape=(
            jax.ShapeDtypeStruct((8, D), F32),
            jax.ShapeDtypeStruct((16, 2048), F32),
        ),
        in_specs=[vm] * 2,
        out_specs=(vm, vm),
        scratch_shapes=[
            pltpu.VMEM((512, 1024), BF16),
            pltpu.VMEM((1024, 1024), F32),
            pltpu.VMEM((3, 32, 2, 16, 1024), BF16),
            pltpu.VMEM((3, 32, 16, 1024), BF16),
            pltpu.VMEM((3, NY, NZ, 16, 1024), BF16),
            pltpu.VMEM((3, NZ, 16, 512), BF16),
            pltpu.VMEM((3, NZ, 16, 512), BF16),
            pltpu.VMEM((3, NZ, 16, 1024), BF16),
            pltpu.VMEM((3, NZ, 16, 1024), BF16),
            pltpu.VMEM((3, NZ, 16, 1024), BF16),
            pltpu.VMEM((3, NZ, 16, 1024), BF16),
            pltpu.VMEM((3, NZ, 16, 1024), BF16),
            pltpu.VMEM((3, NZ, 16, 1024), BF16),
            pltpu.VMEM((16, 1024), F32),
            pltpu.VMEM((16, 1024), F32),
            pltpu.VMEM((24, D), F32),
            pltpu.VMEM((24, D), F32),
            pltpu.VMEM((NZ, 24, D), F32),
            pltpu.VMEM((NY, 24, D), F32),
            pltpu.VMEM((8, D), F32),
            pltpu.VMEM((8, D), F32),
            dma, dma, dma((3,)), dma((3,)), dma((3, 2)), dma((3, 2)), dma((3, 2)), dma((3, 2)),
            dma((3, NZ)), dma((3, NZ)), dma, dma, dma, dma, dma((NZ,)), dma((NZ,)), dma((NY,)), dma((NY,)), dma, dma,
        ],
        compiler_params=pltpu.CompilerParams(
            collective_id=1, has_side_effects=True, vmem_limit_bytes=60 * 1024 * 1024
        ),
        name="gram",
    )(centered, stats)


def body(queries, keys, values, log_decay, gain):
    centered, stats = attend(queries, keys, values, log_decay, gain)
    shift, covariance = gram(centered, stats)
    return (shift.reshape(-1), covariance)


def solution(mesh):
    placed = (P("ctx", "head"), P("ctx", "head"), P("ctx", "head"), P("head", "ctx"), P("head"))
    return jax.shard_map(
        body,
        mesh=mesh,
        in_specs=placed,
        out_specs=(P("head"), P(("head", "ctx"), None)),
        check_vma=False,
    )
```

```python
import functools

import jax
import jax.numpy as jnp
from jax import lax
from jax.experimental import pallas as pl
from jax.experimental.pallas import tpu as pltpu
from jax.sharding import PartitionSpec as P

D = 128
SPAN = 256
NZ = 8
NY = 4
F32 = jnp.float32
BF16 = jnp.bfloat16
MESH = pl.DeviceIdType.MESH
TOK = (((0,), (0,)), ((), ()))
LAST = (((1,), (1,)), ((), ()))


def place():
    me = lax.axis_index("ctx")
    core = lax.rem(me, 2)
    z = lax.rem(me // 2, NZ)
    y = me // (2 * NZ)
    return y, z, core


def at(y, z, core):
    return {"ctx": (y * NZ + z) * 2 + core}


def greet(peers):
    barrier = pltpu.get_barrier_semaphore()
    for peer in peers:
        pl.semaphore_signal(barrier, inc=1, device_id=peer, device_id_type=MESH)
    return lambda: pl.semaphore_wait(barrier, len(peers))


def send(src, dst, ssem, rsem, peer):
    copy = pltpu.make_async_remote_copy(
        src_ref=src, dst_ref=dst, send_sem=ssem, recv_sem=rsem, device_id=peer, device_id_type=MESH
    )
    copy.start()
    return copy


def arrived(src, dst, ssem, rsem, peer):
    pltpu.make_async_remote_copy(
        src_ref=src, dst_ref=dst, send_sem=ssem, recv_sem=rsem, device_id=peer, device_id_type=MESH
    ).wait_recv()


def plane_peers(y, z, core):
    peers = [at(y, z, 1 - core)]
    peers += [at(y, lax.rem(z + i, NZ), core) for i in range(1, NZ)]
    peers += [at(lax.rem(y + i, NY), z, core) for i in range(1, NY)]
    return peers


def expand(piece):
    return jnp.concatenate(
        [jnp.broadcast_to(piece[64 + i : 65 + i], (16, D)) for i in range(4)], axis=0
    )


def join(first, second):
    return expand(second) * first[:64] + second[:64], first[64:] * second[64:]


def attend_kernel(
    q_ref, k_ref, v_ref, ld_ref, gain_ref, c_ref, st_ref,
    cum, col, inner, upd, part, other, chip, zin, pre, yin, back, chipin, give, sin,
    s_core, r_core, s_z, r_z, s_y, r_y, s_zb, r_zb, s_cb, r_cb,
):
    y, z, core = place()
    ready = greet(plane_peers(y, z, core))
    mate = at(y, z, 1 - core)

    total = ld_ref[...]
    lane = lax.rem(lax.broadcasted_iota(jnp.int32, total.shape, 1), SPAN)
    step = 1
    while step < SPAN:
        total = total + jnp.where(lane >= step, pltpu.roll(total, step, 1), 0.0)
        step *= 2
    cum[...] = total
    turned = jnp.transpose(total)
    for head in range(8):
        col[head] = jnp.broadcast_to(turned[:, head : head + 1], (4 * SPAN, D))
    part[...] = jnp.zeros_like(part)

    def lanes(head):
        return pl.ds(pl.multiple_of(head * D, D), D)

    def update(head):
        ending = jnp.zeros((D, D), F32)
        decay = jnp.zeros((1, D), F32)
        for b in range(4):
            rows = pl.ds(b * SPAN, SPAN)
            last = col[head, pl.ds(b * SPAN + SPAN - 1, 1), :]
            scaled = v_ref[rows, lanes(head)].astype(F32) * jnp.exp(last - col[head, rows, :])
            high = scaled.astype(BF16)
            low = (scaled - high.astype(F32)).astype(BF16)
            both = lax.dot_general(
                k_ref[rows, lanes(head)],
                jnp.concatenate([high, low], axis=1),
                TOK,
                preferred_element_type=F32,
            )
            new = both[:, :D] + both[:, D:]
            upd[head, b] = new
            ending = jnp.exp(last) * ending + new
            decay = decay + last
        half, local = head // 4, lax.rem(head, 4)
        for owner in range(NZ):
            part[half, owner, pl.ds(pl.multiple_of(local * 16, 16), 16), :] = ending[
                owner * 16 : owner * 16 + 16
            ]
            part[half, owner, pl.ds(64 + local, 1), :] = jnp.exp(decay)

    later = lax.broadcasted_iota(jnp.int32, (SPAN, SPAN), 0) >= lax.broadcasted_iota(
        jnp.int32, (SPAN, SPAN), 1
    )

    def within(head):
        for b in range(4):
            rows = pl.ds(b * SPAN, SPAN)
            value = v_ref[rows, lanes(head)]
            scores = lax.dot_general(
                q_ref[rows, lanes(head)], k_ref[rows, lanes(head)], LAST, preferred_element_type=F32
            )
            mine = col[head, rows, :]
            diff = jnp.concatenate([mine, mine], axis=1) - cum[pl.ds(head, 1), rows]
            weights = jnp.where(later, scores * jnp.exp(jnp.minimum(diff, 0.0)), 0.0)
            inner[head, rows, :] = jnp.dot(weights.astype(BF16), value, preferred_element_type=F32)

    def loop(lo, hi, work, shift=0):
        def turn(i, carry):
            work(lax.rem(i + shift, 8))
            return carry

        lax.fori_loop(lo, hi, turn, 0)

    loop(0, 4, update, 4 * (1 - core))
    ready()
    out = [send(part.at[1 - core], other, s_core, r_core, mate)]
    loop(4, 8, update, 4 * (1 - core))
    loop(0, 1, within)
    out[0].wait_recv()

    def combine(owner, carry):
        mine, theirs = part[core, owner], other[owner]
        first = jnp.where(core == 0, mine, theirs)
        second = jnp.where(core == 0, theirs, mine)
        state, decay = join(first, second)
        chip[owner, :64, :] = state
        chip[owner, 64:, :] = decay
        return carry

    lax.fori_loop(0, NZ, combine, 0)
    for i in range(1, NZ):
        to = lax.rem(z + i, NZ)
        out.append(send(chip.at[to], zin.at[z], s_z.at[i], r_z.at[z], at(y, to, core)))
    zin[z] = chip[z]
    loop(1, 4, within)
    for i in range(1, NZ):
        frm = lax.rem(z + i, NZ)
        arrived(chip.at[frm], zin.at[frm], s_z.at[i], r_z.at[frm], at(y, frm, core))
    state, decay = jnp.zeros((64, D), F32), jnp.ones((8, D), F32)
    for j in range(NZ):
        pre[j, :64, :] = state
        pre[j, 64:, :] = decay
        state, decay = join(jnp.concatenate([state, decay], axis=0), zin[j])
    yin[y, :64, :] = state
    yin[y, 64:, :] = decay
    for i in range(1, NY):
        to = lax.rem(y + i, NY)
        out.append(send(yin.at[y], yin.at[y], s_y.at[i], r_y.at[y], at(to, z, core)))
    loop(4, 5, within)
    for i in range(1, NY):
        frm = lax.rem(y + i, NY)
        arrived(yin.at[frm], yin.at[frm], s_y.at[i], r_y.at[frm], at(frm, z, core))
    row = jnp.zeros((64, D), F32)
    for j in range(NY):
        piece = yin[j]
        row = jnp.where(j < y, expand(piece) * row + piece[:64], row)
    for j in range(NZ):
        piece = pre[j]
        back[j] = expand(piece) * row + piece[:64]
    for i in range(1, NZ):
        to = lax.rem(z + i, NZ)
        out.append(send(back.at[to], chipin.at[z], s_zb.at[i], r_zb.at[z], at(y, to, core)))
    chipin[z] = back[z]
    loop(5, 8, within)
    for i in range(1, NZ):
        frm = lax.rem(z + i, NZ)
        arrived(back.at[frm], chipin.at[frm], s_zb.at[i], r_zb.at[frm], at(y, frm, core))

    def split(owner, carry):
        lead = jnp.where(core == 0, part[core, owner], other[owner])
        early = chipin[owner]
        late = expand(lead) * early + lead[:64]
        give[owner] = jnp.where(core == 0, late, early)
        sin[core, owner] = jnp.where(core == 0, early, late)
        return carry

    lax.fori_loop(0, NZ, split, 0)
    out.append(send(give, sin.at[core], s_cb, r_cb, mate))

    def finish(head):
        half, local = head // 4, lax.rem(head, 4)
        state = jnp.concatenate(
            [sin[half, owner, pl.ds(pl.multiple_of(local * 16, 16), 16), :] for owner in range(NZ)],
            axis=0,
        )
        gain = gain_ref[pl.ds(head, 1), :]
        mean = jnp.zeros((1, D), F32)
        top = bottom = None
        made = []
        for b in range(4):
            rows = pl.ds(b * SPAN, SPAN)
            high = state.astype(BF16)
            low = (state - high.astype(F32)).astype(BF16)
            both = jnp.dot(
                q_ref[rows, lanes(head)],
                jnp.concatenate([high, low], axis=1),
                preferred_element_type=F32,
            )
            raw = inner[head, rows, :] + jnp.exp(col[head, rows, :]) * (both[:, :D] + both[:, D:])
            scale = jnp.sqrt(jnp.mean(raw * raw, axis=1, keepdims=True) + 1e-06)
            done = (raw / scale * gain).astype(BF16).astype(F32)
            mean = mean + jnp.sum(done, axis=0, keepdims=True)
            high_b = jnp.max(done, axis=0, keepdims=True)
            low_b = jnp.min(done, axis=0, keepdims=True)
            top = high_b if top is None else jnp.maximum(top, high_b)
            bottom = low_b if bottom is None else jnp.minimum(bottom, low_b)
            made.append(done)
            inner[head, rows, :] = done
            if b < 3:
                last = col[head, pl.ds(b * SPAN + SPAN - 1, 1), :]
                state = jnp.exp(last) * state + upd[head, b]
        mean = mean / (4 * SPAN)
        for b in range(4):
            rows = pl.ds(b * SPAN, SPAN)
            c_ref[rows, lanes(head)] = (inner[head, rows, :] - mean).astype(BF16)
        st_ref[pl.ds(head, 1), :] = mean
        st_ref[pl.ds(8 + head, 1), :] = top
        st_ref[pl.ds(16 + head, 1), :] = bottom

    loop(0, 4, finish, 4 * core)
    out[-1].wait_recv()
    loop(4, 8, finish, 4 * core)
    for copy in out:
        copy.wait_send()


def attend(q, k, v, log_decay, gain):
    count, width = q.shape
    vm = pl.BlockSpec(memory_space=pltpu.VMEM)
    dma = pltpu.SemaphoreType.DMA
    return pl.pallas_call(
        attend_kernel,
        out_shape=(
            jax.ShapeDtypeStruct((count, width), BF16),
            jax.ShapeDtypeStruct((24, D), F32),
        ),
        in_specs=[vm] * 5,
        out_specs=(vm, vm),
        scratch_shapes=[
            pltpu.VMEM((8, 1024), F32),
            pltpu.VMEM((8, 1024, D), F32),
            pltpu.VMEM((8, 1024, D), F32),
            pltpu.VMEM((8, 4, D, D), F32),
            pltpu.VMEM((2, NZ, 72, D), F32),
            pltpu.VMEM((NZ, 72, D), F32),
            pltpu.VMEM((NZ, 72, D), F32),
            pltpu.VMEM((NZ, 72, D), F32),
            pltpu.VMEM((NZ, 72, D), F32),
            pltpu.VMEM((NY, 72, D), F32),
            pltpu.VMEM((NZ, 64, D), F32),
            pltpu.VMEM((NZ, 64, D), F32),
            pltpu.VMEM((NZ, 64, D), F32),
            pltpu.VMEM((2, NZ, 64, D), F32),
            dma, dma, dma((NZ,)), dma((NZ,)), dma((NY,)), dma((NY,)), dma((NZ,)), dma((NZ,)), dma, dma,
        ],
        compiler_params=pltpu.CompilerParams(
            collective_id=0, has_side_effects=True, vmem_limit_bytes=60 * 1024 * 1024
        ),
        name="attend",
    )(q, k, v, log_decay, gain.reshape(8, D))


WIDE = 512
SEGS = 6


def gram_kernel(
    c_ref, st_ref, shift_ref, cov_ref,
    theirs, grams, mates, sums, ylow, yhigh, yfirst, ylast, ynext, yprev, zsend, zin, strip, hop,
    means, ar, armate, stz, sty, left, right,
    s_m, r_m, s_x, r_x, s_c, r_c, s_y1, r_y1, s_y2, r_y2, s_z, r_z, s_h, r_h,
    s_s1, r_s1, s_sz, r_sz, s_sy, r_sy, s_g, r_g,
):
    y, z, core = place()
    parity = lax.rem(lax.axis_index("head"), 2)
    pair = {"head": lax.axis_index("head") + 1 - 2 * parity}
    mate = at(y, z, 1 - core)
    north, south = lax.rem(y + 1, NY), lax.rem(y + NY - 1, NY)
    far = lax.rem(y + 2, NY)
    ready = greet(plane_peers(y, z, core) + [pair])
    ready()
    out = []

    def keep(copy):
        out.append(copy)
        return copy

    other_half = pl.ds(pl.multiple_of((1 - parity) * 512, 512), 512)
    half = pl.ds(pl.multiple_of(parity * 512, 512), 512)
    swap_mean = keep(send(st_ref.at[pl.ds(0, 8)], means.at[y, core, pl.ds(8, 8)], s_m, r_m, pair))
    swaps = [
        keep(
            send(c_ref.at[other_half, pl.ds(k * WIDE, WIDE)], theirs.at[k], s_x.at[k], r_x.at[k], pair)
        )
        for k in range(2)
    ]
    means[y, core, :8, :] = st_ref[:8, :]

    def store(seg, first, value):
        count = value.shape[0] // 32
        grams[seg, pl.ds(first // 32, count)] = value.astype(BF16).reshape(count, 2, 16, WIDE)

    def to_mate(seg):
        return keep(send(grams.at[seg, :, 1 - core], mates.at[seg], s_c.at[seg], r_c.at[seg], mate))

    def start_diag(k):
        for i in range(4):
            store(
                k,
                i * 256,
                lax.dot_general(
                    c_ref[:, i * 256 : i * 256 + 256],
                    c_ref[:, k * WIDE : k * WIDE + WIDE],
                    TOK,
                    preferred_element_type=F32,
                ),
            )
        return to_mate(k)

    def start_cross(k):
        for i in range(4):
            store(
                2 + k,
                i * 256,
                lax.dot_general(
                    c_ref[half, i * 256 : i * 256 + 256], theirs[k], TOK, preferred_element_type=F32
                ),
            )
        return to_mate(2 + k)

    def start_turned(k):
        for i in range(4):
            store(
                4 + k,
                i * 256,
                lax.dot_general(
                    theirs[i // 2, :, (i % 2) * 256 : (i % 2) * 256 + 256],
                    c_ref[half, k * WIDE : k * WIDE + WIDE],
                    TOK,
                    preferred_element_type=F32,
                ),
            )
        return to_mate(4 + k)

    def merge(a, b):
        return jnp.concatenate(
            [a[:16] + b[:16], jnp.maximum(a[16:24], b[16:24]), jnp.minimum(a[24:], b[24:])], axis=0
        )

    def add_mate(seg, copy):
        copy.wait_recv()

        def turn(i, carry):
            four = pl.ds(i * 4, 4)
            got = grams[seg, four, core].astype(F32) + mates[seg, four].astype(F32)
            sums[seg, four] = got.astype(BF16)
            return carry

        lax.fori_loop(0, NZ, turn, 0)
        part = sums.at[seg, pl.ds(far * NZ, NZ)]
        edge = WIDE // 2
        up = keep(
            send(part.at[:, :, pl.ds(0, edge)], ylow.at[seg], s_y1.at[seg, 0], r_y1.at[seg, 0], at(north, z, core))
        )
        down = keep(
            send(part.at[:, :, pl.ds(edge, edge)], yhigh.at[seg], s_y1.at[seg, 1], r_y1.at[seg, 1], at(south, z, core))
        )
        return up, down

    def pass_on(seg, copies):
        copies[0].wait_recv()
        copies[1].wait_recv()
        edge = WIDE // 2

        def turn(i, carry):
            two = pl.ds(i * 2, 2)
            a = sums[seg, pl.ds(north * NZ + i * 2, 2)]
            b = sums[seg, pl.ds(south * NZ + i * 2, 2)]
            low = a[:, :, :edge].astype(F32) + ylow[seg, two].astype(F32)
            high = b[:, :, edge:].astype(F32) + yhigh[seg, two].astype(F32)
            ynext[seg, two, :, :edge] = low.astype(BF16)
            ynext[seg, two, :, edge:] = a[:, :, edge:]
            yprev[seg, two, :, :edge] = b[:, :, :edge]
            yprev[seg, two, :, edge:] = high.astype(BF16)
            return carry

        lax.fori_loop(0, 4, turn, 0)
        up = keep(send(ynext.at[seg], yfirst.at[seg], s_y2.at[seg, 0], r_y2.at[seg, 0], at(north, z, core)))
        down = keep(send(yprev.at[seg], ylast.at[seg], s_y2.at[seg, 1], r_y2.at[seg, 1], at(south, z, core)))
        return up, down

    def to_z(seg, copies):
        copies[0].wait_recv()
        copies[1].wait_recv()
        tall = 1024 if seg >= 4 else 0
        wide = (1024 if seg in (2, 3) else 0) + (seg % 2) * WIDE
        weight = 1024.0 if seg < 2 else 512.0
        spread = weight * lax.dot_general(
            left[:, pl.ds(pl.multiple_of(tall + y * 256, 256), 256)],
            right[:, wide : wide + WIDE],
            TOK,
            preferred_element_type=F32,
        )
        spread = spread.reshape(NZ, 2, 16, WIDE)
        spread = jnp.where(core == 0, spread[:, 0], spread[:, 1])
        got = sums[seg, pl.ds(y * NZ, NZ)].astype(F32) + yfirst[seg].astype(F32)
        got = got + ylast[seg].astype(F32) + spread
        zsend[seg] = got.astype(BF16)
        for i in range(1, NZ):
            to = lax.rem(z + i, NZ)
            keep(
                send(zsend.at[seg, to], zin.at[seg, z], s_z.at[seg, i], r_z.at[seg, z], at(y, to, core))
            )
        zin[seg, z] = zsend[seg, z]

    def from_z(seg):
        for i in range(1, NZ):
            frm = lax.rem(z + i, NZ)
            arrived(
                zsend.at[seg, frm], zin.at[seg, frm], s_z.at[seg, i], r_z.at[seg, frm], at(y, frm, core)
            )
        got = zin[seg, 0].astype(F32)
        for j in range(1, NZ):
            got = got + zin[seg, j].astype(F32)
        return got

    c0 = start_diag(0)
    swap_mean.wait_recv()
    ar[:16, :] = means[y, core]
    ar[16:, :] = st_ref[8:, :]
    first = keep(send(ar, armate, s_s1, r_s1, mate))
    c1 = start_diag(1)
    first.wait_recv()
    means[y, 1 - core] = armate[:16, :]
    stz[z] = merge(ar[...], armate[...])
    for i in range(1, NZ):
        to = lax.rem(z + i, NZ)
        keep(send(stz.at[z], stz.at[z], s_sz.at[i], r_sz.at[z], at(y, to, core)))
    for i in range(1, NY):
        to = lax.rem(y + i, NY)
        keep(send(means.at[y], means.at[y], s_g.at[i], r_g.at[y], at(to, z, core)))
    p0 = add_mate(0, c0)
    p1 = add_mate(1, c1)
    for i in range(1, NZ):
        frm = lax.rem(z + i, NZ)
        arrived(stz.at[frm], stz.at[frm], s_sz.at[i], r_sz.at[frm], at(y, frm, core))
    sty[y] = functools.reduce(merge, [stz[j] for j in range(NZ)])
    for i in range(1, NY):
        to = lax.rem(y + i, NY)
        keep(send(sty.at[y], sty.at[y], s_sy.at[i], r_sy.at[y], at(to, z, core)))
    q0 = pass_on(0, p0)
    q1 = pass_on(1, p1)
    for i in range(1, NY):
        frm = lax.rem(y + i, NY)
        arrived(means.at[frm], means.at[frm], s_g.at[i], r_g.at[frm], at(frm, z, core))
        arrived(sty.at[frm], sty.at[frm], s_sy.at[i], r_sy.at[frm], at(frm, z, core))
    every = functools.reduce(merge, [sty[j] for j in range(NY)])
    shift_ref[...] = (every[16:24] + every[24:]) / 2.0
    mu = every[:16] / 64.0
    off = means[...].reshape(NY * 2, 16, D) - mu[None]
    for j in range(16):
        piece = off[:, j, :]
        high = piece.astype(BF16)
        low = (piece - high.astype(F32)).astype(BF16)
        none = jnp.zeros_like(high)
        cols = slice(j * D, j * D + D)
        left[:, cols] = jnp.concatenate([high, high, low, none], axis=0)
        right[:, cols] = jnp.concatenate([high, low, high, none], axis=0)
    swaps[0].wait_recv()
    c2 = start_cross(0)
    to_z(0, q0)
    p2 = add_mate(2, c2)
    to_z(1, q1)
    q2 = pass_on(2, p2)
    swaps[1].wait_recv()
    c4 = start_turned(0)
    c5 = start_turned(1)
    p4 = add_mate(4, c4)
    c3 = start_cross(1)
    p5 = add_mate(5, c5)
    to_z(2, q2)
    q4 = pass_on(4, p4)
    p3 = add_mate(3, c3)
    diag0 = from_z(0)
    diag1 = from_z(1)
    diag = jnp.concatenate([diag0, diag1], axis=1) / 65536.0
    q5 = pass_on(5, p5)
    to_z(4, q4)
    q3 = pass_on(3, p3)
    cross0 = from_z(2)
    to_z(5, q5)
    strip[0] = from_z(4)
    hop0 = keep(send(strip.at[0], hop.at[0], s_h.at[0], r_h.at[0], pair))
    to_z(3, q3)
    strip[1] = from_z(5)
    hop1 = keep(send(strip.at[1], hop.at[1], s_h.at[1], r_h.at[1], pair))
    cross1 = from_z(3)
    hop0.wait_recv()
    hop1.wait_recv()
    cross = jnp.concatenate([cross0 + hop[0], cross1 + hop[1]], axis=1) / 65536.0
    cov_ref[:, :1024] = jnp.where(parity == 0, diag, cross)
    cov_ref[:, 1024:] = jnp.where(parity == 0, cross, diag)
    for copy in out:
        copy.wait_send()


def gram(centered, stats):
    vm = pl.BlockSpec(memory_space=pltpu.VMEM)
    dma = pltpu.SemaphoreType.DMA
    block = pltpu.VMEM((SEGS, NZ, 16, WIDE), BF16)
    edge = pltpu.VMEM((SEGS, NZ, 16, WIDE // 2), BF16)
    return pl.pallas_call(
        gram_kernel,
        out_shape=(
            jax.ShapeDtypeStruct((8, D), F32),
            jax.ShapeDtypeStruct((16, 2048), F32),
        ),
        in_specs=[vm] * 2,
        out_specs=(vm, vm),
        scratch_shapes=[
            pltpu.VMEM((2, 512, WIDE), BF16),
            pltpu.VMEM((SEGS, 32, 2, 16, WIDE), BF16),
            pltpu.VMEM((SEGS, 32, 16, WIDE), BF16),
            pltpu.VMEM((SEGS, 32, 16, WIDE), BF16),
            edge, edge, block, block, block, block, block, block,
            pltpu.VMEM((2, 16, WIDE), F32),
            pltpu.VMEM((2, 16, WIDE), F32),
            pltpu.VMEM((NY, 2, 16, D), F32),
            pltpu.VMEM((32, D), F32),
            pltpu.VMEM((32, D), F32),
            pltpu.VMEM((NZ, 32, D), F32),
            pltpu.VMEM((NY, 32, D), F32),
            pltpu.VMEM((32, 2048), BF16),
            pltpu.VMEM((32, 2048), BF16),
            dma, dma, dma((2,)), dma((2,)), dma((SEGS,)), dma((SEGS,)),
            dma((SEGS, 2)), dma((SEGS, 2)), dma((SEGS, 2)), dma((SEGS, 2)),
            dma((SEGS, NZ)), dma((SEGS, NZ)), dma((2,)), dma((2,)),
            dma, dma, dma((NZ,)), dma((NZ,)), dma((NY,)), dma((NY,)), dma((NY,)), dma((NY,)),
        ],
        compiler_params=pltpu.CompilerParams(
            collective_id=1, has_side_effects=True, vmem_limit_bytes=60 * 1024 * 1024
        ),
        name="gram",
    )(centered, stats)


def hand_kernel(a_ref, b_ref, c_ref, d_ref):
    c_ref[...] = a_ref[...]
    d_ref[...] = b_ref[...]


def hand_out(shift, covariance):
    vm = pl.BlockSpec(memory_space=pltpu.VMEM)
    return pl.pallas_call(
        hand_kernel,
        out_shape=(
            jax.ShapeDtypeStruct(shift.shape, F32),
            jax.ShapeDtypeStruct(covariance.shape, F32),
        ),
        in_specs=[vm] * 2,
        out_specs=(vm, vm),
        name="hand_out",
    )(shift, covariance)


def body(queries, keys, values, log_decay, gain):
    centered, stats = attend(queries, keys, values, log_decay, gain)
    shift, covariance = hand_out(*gram(centered, stats))
    return (shift.reshape(-1), covariance)


def solution(mesh):
    placed = (P("ctx", "head"), P("ctx", "head"), P("ctx", "head"), P("head", "ctx"), P("head"))
    return jax.shard_map(
        body,
        mesh=mesh,
        in_specs=placed,
        out_specs=(P("head"), P(("head", "ctx"), None)),
        check_vma=False,
    )
```

```python
import functools

import jax
import jax.numpy as jnp
from jax import lax
from jax.experimental import pallas as pl
from jax.experimental.pallas import tpu as pltpu
from jax.sharding import PartitionSpec as P

D = 128
SPAN = 256
NZ = 8
NY = 4
F32 = jnp.float32
BF16 = jnp.bfloat16
MESH = pl.DeviceIdType.MESH
TOK = (((0,), (0,)), ((), ()))
LAST = (((1,), (1,)), ((), ()))


def place():
    me = lax.axis_index("ctx")
    core = lax.rem(me, 2)
    z = lax.rem(me // 2, NZ)
    y = me // (2 * NZ)
    return y, z, core


def at(y, z, core):
    return {"ctx": (y * NZ + z) * 2 + core}


def greet(peers):
    barrier = pltpu.get_barrier_semaphore()
    for peer in peers:
        pl.semaphore_signal(barrier, inc=1, device_id=peer, device_id_type=MESH)
    return lambda: pl.semaphore_wait(barrier, len(peers))


def send(src, dst, ssem, rsem, peer):
    copy = pltpu.make_async_remote_copy(
        src_ref=src, dst_ref=dst, send_sem=ssem, recv_sem=rsem, device_id=peer, device_id_type=MESH
    )
    copy.start()
    return copy


def arrived(src, dst, ssem, rsem, peer):
    pltpu.make_async_remote_copy(
        src_ref=src, dst_ref=dst, send_sem=ssem, recv_sem=rsem, device_id=peer, device_id_type=MESH
    ).wait_recv()


def plane_peers(y, z, core):
    peers = [at(y, z, 1 - core)]
    peers += [at(y, lax.rem(z + i, NZ), core) for i in range(1, NZ)]
    peers += [at(lax.rem(y + i, NY), z, core) for i in range(1, NY)]
    return peers


PIECE = 32
DIAG, CROSS, TURNED = 0, 1, 2
SEGMENTS = (
    (DIAG, 0, 512),
    (DIAG, 512, 512),
    (CROSS, 0, 512),
    (CROSS, 512, 256),
    (TURNED, 0, 512),
    (TURNED, 512, 512),
    (CROSS, 768, 256),
)
SEGS = len(SEGMENTS)


def expand(piece):
    return jnp.concatenate(
        [jnp.broadcast_to(piece[PIECE + i : PIECE + i + 1], (16, D)) for i in range(2)], axis=0
    )


def join(first, second):
    return expand(second) * first[:PIECE] + second[:PIECE], first[PIECE:] * second[PIECE:]


def kernel(
    q_hbm, k_hbm, v_hbm, ld_ref, gain_ref, shift_ref, cov_ref,
    q_ref, k_ref, v_ref, c_ref, st_ref,
    cum, col, inner, upd, part, other, chip, zin, pre, yin, back, chipin, give, sin,
    theirs, strip, hop, means, armate, stz, sty, off, offin, left, right,
    grams, mates, sums, ylow, yhigh, yfirst, ylast, ynext, yprev, zsend, zgot,
    s_in, s_core, r_core, s_z, r_z, s_y, r_y, s_zb, r_zb, s_cb, r_cb,
    s_m, r_m, s_x, r_x, s_c, r_c, s_y1, r_y1, s_y2, r_y2, s_zz, r_zz, s_h, r_h,
    s_s1, r_s1, s_sz, r_sz, s_sy, r_sy, s_g, r_g,
):
    y, z, core = place()
    parity = lax.rem(lax.axis_index("head"), 2)
    pair = {"head": lax.axis_index("head") + 1 - 2 * parity}
    mate = at(y, z, 1 - core)
    north, south = lax.rem(y + 1, NY), lax.rem(y + NY - 1, NY)
    far = lax.rem(y + 2, NY)
    ready = greet(plane_peers(y, z, core) + [pair])
    out = []

    def keep(copy):
        out.append(copy)
        return copy

    def load(src, dst, sem):
        copy = pltpu.make_async_copy(src, dst, sem)
        copy.start()
        return copy

    def half_of(ref, g):
        return ref.at[:, pl.ds(g * 512, 512)]

    kv_in = [
        (
            load(half_of(k_hbm, g), half_of(k_ref, g), s_in.at[2 * g]),
            load(half_of(v_hbm, g), half_of(v_ref, g), s_in.at[2 * g + 1]),
        )
        for g in range(2)
    ]
    q_in = load(q_hbm, q_ref, s_in.at[4])

    total = ld_ref[...]
    lane = lax.rem(lax.broadcasted_iota(jnp.int32, total.shape, 1), SPAN)
    step = 1
    while step < SPAN:
        total = total + jnp.where(lane >= step, pltpu.roll(total, step, 1), 0.0)
        step *= 2
    cum[...] = total
    turned = jnp.transpose(total)
    for head in range(8):
        col[head] = jnp.broadcast_to(turned[:, head : head + 1], (4 * SPAN, D))
    part[...] = jnp.zeros_like(part)

    def lanes(head):
        return pl.ds(pl.multiple_of(head * D, D), D)

    def both_heads(work):
        def turn(i, carry):
            work(i)
            return carry

        lax.fori_loop(0, 2, turn, 0)

    def update(g, owning):
        def one(i):
            head = 4 * g + 2 * owning + i
            ending = jnp.zeros((D, D), F32)
            decay = jnp.zeros((1, D), F32)
            for b in range(4):
                rows = pl.ds(b * SPAN, SPAN)
                last = col[head, pl.ds(b * SPAN + SPAN - 1, 1), :]
                scaled = v_ref[rows, lanes(head)].astype(F32) * jnp.exp(last - col[head, rows, :])
                high = scaled.astype(BF16)
                low = (scaled - high.astype(F32)).astype(BF16)
                both = lax.dot_general(
                    k_ref[rows, lanes(head)],
                    jnp.concatenate([high, low], axis=1),
                    TOK,
                    preferred_element_type=F32,
                )
                new = both[:, :D] + both[:, D:]
                upd[head, b] = new
                ending = jnp.exp(last) * ending + new
                decay = decay + last
            for owner in range(NZ):
                part[g, owning, owner, pl.ds(pl.multiple_of(i * 16, 16), 16), :] = ending[
                    owner * 16 : owner * 16 + 16
                ]
                part[g, owning, owner, pl.ds(PIECE + i, 1), :] = jnp.exp(decay)

        both_heads(one)

    later = lax.broadcasted_iota(jnp.int32, (SPAN, SPAN), 0) >= lax.broadcasted_iota(
        jnp.int32, (SPAN, SPAN), 1
    )

    def within(lo, hi):
        def turn(head, carry):
            for b in range(4):
                rows = pl.ds(b * SPAN, SPAN)
                scores = lax.dot_general(
                    q_ref[rows, lanes(head)],
                    k_ref[rows, lanes(head)],
                    LAST,
                    preferred_element_type=F32,
                )
                mine = col[head, rows, :]
                diff = jnp.concatenate([mine, mine], axis=1) - cum[pl.ds(head, 1), rows]
                weights = jnp.where(later, scores * jnp.exp(jnp.minimum(diff, 0.0)), 0.0)
                inner[head, rows, :] = jnp.dot(
                    weights.astype(BF16), v_ref[rows, lanes(head)], preferred_element_type=F32
                )
            return carry

        lax.fori_loop(lo, hi, turn, 0)

    def to_core(g):
        return keep(send(part.at[g, 1 - core], other.at[g], s_core.at[g], r_core.at[g], mate))

    def to_owners(g, copy):
        copy.wait_recv()

        def combine(owner, carry):
            mine, theirs_ = part[g, core, owner], other[g, owner]
            first = jnp.where(core == 0, mine, theirs_)
            second = jnp.where(core == 0, theirs_, mine)
            state, decay = join(first, second)
            chip[g, owner, :PIECE, :] = state
            chip[g, owner, PIECE:, :] = decay
            return carry

        lax.fori_loop(0, NZ, combine, 0)
        for i in range(1, NZ):
            to = lax.rem(z + i, NZ)
            keep(send(chip.at[g, to], zin.at[g, z], s_z.at[g, i], r_z.at[g, z], at(y, to, core)))
        zin[g, z] = chip[g, z]

    def to_rows(g):
        for i in range(1, NZ):
            frm = lax.rem(z + i, NZ)
            arrived(chip.at[g, frm], zin.at[g, frm], s_z.at[g, i], r_z.at[g, frm], at(y, frm, core))
        state, decay = jnp.zeros((PIECE, D), F32), jnp.ones((8, D), F32)
        for j in range(NZ):
            pre[g, j, :PIECE, :] = state
            pre[g, j, PIECE:, :] = decay
            state, decay = join(jnp.concatenate([state, decay], axis=0), zin[g, j])
        yin[g, y, :PIECE, :] = state
        yin[g, y, PIECE:, :] = decay
        for i in range(1, NY):
            to = lax.rem(y + i, NY)
            keep(send(yin.at[g, y], yin.at[g, y], s_y.at[g, i], r_y.at[g, y], at(to, z, core)))

    def to_chips(g):
        for i in range(1, NY):
            frm = lax.rem(y + i, NY)
            arrived(yin.at[g, frm], yin.at[g, frm], s_y.at[g, i], r_y.at[g, frm], at(frm, z, core))
        row = jnp.zeros((PIECE, D), F32)
        for j in range(NY):
            piece = yin[g, j]
            row = jnp.where(j < y, expand(piece) * row + piece[:PIECE], row)
        for j in range(NZ):
            piece = pre[g, j]
            back[g, j] = expand(piece) * row + piece[:PIECE]
        for i in range(1, NZ):
            to = lax.rem(z + i, NZ)
            keep(send(back.at[g, to], chipin.at[g, z], s_zb.at[g, i], r_zb.at[g, z], at(y, to, core)))
        chipin[g, z] = back[g, z]

    def to_cores(g):
        for i in range(1, NZ):
            frm = lax.rem(z + i, NZ)
            arrived(
                back.at[g, frm], chipin.at[g, frm], s_zb.at[g, i], r_zb.at[g, frm], at(y, frm, core)
            )

        def split(owner, carry):
            lead = jnp.where(core == 0, part[g, core, owner], other[g, owner])
            early = chipin[g, owner]
            late = expand(lead) * early + lead[:PIECE]
            give[g, owner] = jnp.where(core == 0, late, early)
            sin[g, core, owner] = jnp.where(core == 0, early, late)
            return carry

        lax.fori_loop(0, NZ, split, 0)
        return keep(send(give.at[g], sin.at[g, core], s_cb.at[g], r_cb.at[g], mate))

    def finish(g, owning):
        def one(i):
            head = 4 * g + 2 * owning + i
            state = jnp.concatenate(
                [
                    sin[g, owning, owner, pl.ds(pl.multiple_of(i * 16, 16), 16), :]
                    for owner in range(NZ)
                ],
                axis=0,
            )
            gain = gain_ref[pl.ds(head, 1), :]
            mean = jnp.zeros((1, D), F32)
            top = bottom = None
            for b in range(4):
                rows = pl.ds(b * SPAN, SPAN)
                high = state.astype(BF16)
                low = (state - high.astype(F32)).astype(BF16)
                both = jnp.dot(
                    q_ref[rows, lanes(head)],
                    jnp.concatenate([high, low], axis=1),
                    preferred_element_type=F32,
                )
                raw = inner[head, rows, :] + jnp.exp(col[head, rows, :]) * (both[:, :D] + both[:, D:])
                scale = jnp.sqrt(jnp.mean(raw * raw, axis=1, keepdims=True) + 1e-06)
                done = (raw / scale * gain).astype(BF16).astype(F32)
                mean = mean + jnp.sum(done, axis=0, keepdims=True)
                high_b = jnp.max(done, axis=0, keepdims=True)
                low_b = jnp.min(done, axis=0, keepdims=True)
                top = high_b if top is None else jnp.maximum(top, high_b)
                bottom = low_b if bottom is None else jnp.minimum(bottom, low_b)
                inner[head, rows, :] = done
                if b < 3:
                    last = col[head, pl.ds(b * SPAN + SPAN - 1, 1), :]
                    state = jnp.exp(last) * state + upd[head, b]
            mean = mean / (4 * SPAN)
            for b in range(4):
                rows = pl.ds(b * SPAN, SPAN)
                c_ref[rows, lanes(head)] = (inner[head, rows, :] - mean).astype(BF16)
            st_ref[pl.ds(head, 1), :] = mean
            st_ref[pl.ds(8 + head, 1), :] = top
            st_ref[pl.ds(16 + head, 1), :] = bottom

        both_heads(one)

    other_half = pl.ds(pl.multiple_of((1 - parity) * 512, 512), 512)
    half = pl.ds(pl.multiple_of(parity * 512, 512), 512)

    def columns(j):
        return pl.ds(pl.multiple_of(j * 256, 256), 256)

    def to_pair(j):
        return keep(
            send(
                c_ref.at[other_half, columns(j)],
                theirs.at[:, columns(j)],
                s_x.at[j],
                r_x.at[j],
                pair,
            )
        )

    def from_pair(j):
        arrived(
            c_ref.at[other_half, columns(j)], theirs.at[:, columns(j)], s_x.at[j], r_x.at[j], pair
        )

    def to_mate(seg):
        return keep(send(grams[seg].at[:, 1 - core], mates[seg], s_c.at[seg], r_c.at[seg], mate))

    def begin(seg):
        kind, first, wide = SEGMENTS[seg]
        cols = slice(first, first + wide)
        for i in range(4):
            rows = slice(i * 256, i * 256 + 256)
            if kind == DIAG:
                a, b = c_ref[:, rows], c_ref[:, cols]
            elif kind == CROSS:
                a, b = c_ref[half, rows], theirs[:, cols]
            else:
                a, b = theirs[:, rows], c_ref[half, cols]
            value = lax.dot_general(a, b, TOK, preferred_element_type=F32)
            grams[seg][pl.ds(8 * i, 8)] = value.astype(BF16).reshape(8, 2, 16, wide)
        return to_mate(seg)

    def merge(a, b):
        return jnp.concatenate(
            [a[:8] + b[:8], jnp.maximum(a[8:16], b[8:16]), jnp.minimum(a[16:], b[16:])], axis=0
        )

    def add_mate(seg, copy):
        copy.wait_recv()

        def turn(i, carry):
            four = pl.ds(i * 4, 4)
            got = grams[seg][four, core].astype(F32) + mates[seg][four].astype(F32)
            sums[seg][four] = got.astype(BF16)
            return carry

        lax.fori_loop(0, NZ, turn, 0)
        block = sums[seg].at[pl.ds(far * NZ, NZ)]
        edge = SEGMENTS[seg][2] // 2
        up = keep(
            send(block.at[:, :, pl.ds(0, edge)], ylow[seg], s_y1.at[seg, 0], r_y1.at[seg, 0], at(north, z, core))
        )
        down = keep(
            send(block.at[:, :, pl.ds(edge, edge)], yhigh[seg], s_y1.at[seg, 1], r_y1.at[seg, 1], at(south, z, core))
        )
        return up, down

    def pass_on(seg, copies):
        copies[0].wait_recv()
        copies[1].wait_recv()
        edge = SEGMENTS[seg][2] // 2

        def turn(i, carry):
            two = pl.ds(i * 2, 2)
            a = sums[seg][pl.ds(north * NZ + i * 2, 2)]
            b = sums[seg][pl.ds(south * NZ + i * 2, 2)]
            low = a[:, :, :edge].astype(F32) + ylow[seg][two].astype(F32)
            high = b[:, :, edge:].astype(F32) + yhigh[seg][two].astype(F32)
            ynext[seg][two, :, :edge] = low.astype(BF16)
            ynext[seg][two, :, edge:] = a[:, :, edge:]
            yprev[seg][two, :, :edge] = b[:, :, :edge]
            yprev[seg][two, :, edge:] = high.astype(BF16)
            return carry

        lax.fori_loop(0, 4, turn, 0)
        up = keep(send(ynext[seg], yfirst[seg], s_y2.at[seg, 0], r_y2.at[seg, 0], at(north, z, core)))
        down = keep(send(yprev[seg], ylast[seg], s_y2.at[seg, 1], r_y2.at[seg, 1], at(south, z, core)))
        return up, down

    def to_z(seg, copies):
        copies[0].wait_recv()
        copies[1].wait_recv()
        kind, first, wide = SEGMENTS[seg]
        tall = 1024 if kind == TURNED else 0
        start = first + (1024 if kind == CROSS else 0)
        spread = lax.dot_general(
            left[:, pl.ds(pl.multiple_of(tall + y * 256, 256), 256)],
            right[:, start : start + wide],
            TOK,
            preferred_element_type=F32,
        )
        spread = spread.reshape(NZ, 2, 16, wide) * (1024.0 if kind == DIAG else 512.0)
        spread = jnp.where(core == 0, spread[:, 0], spread[:, 1])
        got = sums[seg][pl.ds(y * NZ, NZ)].astype(F32) + yfirst[seg][...].astype(F32)
        got = got + ylast[seg][...].astype(F32) + spread
        zsend[seg][...] = got.astype(BF16)
        for i in range(1, NZ):
            to = lax.rem(z + i, NZ)
            keep(
                send(zsend[seg].at[to], zgot[seg].at[z], s_zz.at[seg, i], r_zz.at[seg, z], at(y, to, core))
            )
        zgot[seg][z] = zsend[seg][z]

    def from_z(seg):
        for i in range(1, NZ):
            frm = lax.rem(z + i, NZ)
            arrived(
                zsend[seg].at[frm], zgot[seg].at[frm], s_zz.at[seg, i], r_zz.at[seg, frm], at(y, frm, core)
            )
        got = zgot[seg][0].astype(F32)
        for j in range(1, NZ):
            got = got + zgot[seg][j].astype(F32)
        return got

    def kv_ready(g):
        kv_in[g][0].wait()
        kv_in[g][1].wait()

    kv_ready(0)
    update(0, 1 - core)
    ready()
    b0 = to_core(0)
    update(0, core)
    kv_ready(1)
    update(1, 1 - core)
    b1 = to_core(1)
    to_owners(0, b0)
    update(1, core)
    to_owners(1, b1)
    q_in.wait()
    within(0, 6)
    to_rows(0)
    within(6, 7)
    to_rows(1)
    within(7, 8)
    to_chips(0)
    to_chips(1)
    e0 = to_cores(0)
    finish(0, core)
    to_pair(core)
    e0.wait_recv()
    finish(0, 1 - core)
    to_pair(1 - core)
    e1 = to_cores(1)
    finish(1, core)
    e1.wait_recv()
    finish(1, 1 - core)
    first = keep(send(st_ref, armate, s_s1, r_s1, mate))
    to_pair(2)
    to_pair(3)
    means[y, core] = st_ref[:8, :]

    def spread_rows(source, base):
        for j in range(8):
            piece = source[:, j, :]
            high = piece.astype(BF16)
            low = (piece - high.astype(F32)).astype(BF16)
            none = jnp.zeros_like(high)
            cols = slice(base + j * D, base + j * D + D)
            left[:, cols] = jnp.concatenate([high, high, low, none], axis=0)
            right[:, cols] = jnp.concatenate([high, low, high, none], axis=0)

    c0 = begin(0)
    first.wait_recv()
    means[y, 1 - core] = armate[:8, :]
    stz[z] = merge(st_ref[...], armate[...])
    for i in range(1, NZ):
        to = lax.rem(z + i, NZ)
        keep(send(stz.at[z], stz.at[z], s_sz.at[i], r_sz.at[z], at(y, to, core)))
    for i in range(1, NY):
        to = lax.rem(y + i, NY)
        keep(send(means.at[y], means.at[y], s_g.at[i], r_g.at[y], at(to, z, core)))
    c1 = begin(1)
    p0 = add_mate(0, c0)
    p1 = add_mate(1, c1)
    q0 = pass_on(0, p0)
    from_pair(core)
    from_pair(1 - core)
    c2 = begin(2)
    q1 = pass_on(1, p1)
    for i in range(1, NZ):
        frm = lax.rem(z + i, NZ)
        arrived(stz.at[frm], stz.at[frm], s_sz.at[i], r_sz.at[frm], at(y, frm, core))
    sty[y] = functools.reduce(merge, [stz[j] for j in range(NZ)])
    for i in range(1, NY):
        to = lax.rem(y + i, NY)
        keep(send(sty.at[y], sty.at[y], s_sy.at[i], r_sy.at[y], at(to, z, core)))
    p2 = add_mate(2, c2)
    from_pair(2)
    c3 = begin(3)
    for i in range(1, NY):
        frm = lax.rem(y + i, NY)
        arrived(means.at[frm], means.at[frm], s_g.at[i], r_g.at[frm], at(frm, z, core))
        arrived(sty.at[frm], sty.at[frm], s_sy.at[i], r_sy.at[frm], at(frm, z, core))
    every = functools.reduce(merge, [sty[j] for j in range(NY)])
    shift_ref[...] = (every[8:16] + every[16:]) / 2.0
    off[...] = means[...].reshape(NY * 2, 8, D) - (every[:8] / 64.0)[None]
    offset = keep(send(off, offin, s_m, r_m, pair))
    spread_rows(off, 0)
    to_z(0, q0)
    to_z(1, q1)
    q2 = pass_on(2, p2)
    p3 = add_mate(3, c3)
    from_pair(3)
    c4 = begin(4)
    c5 = begin(5)
    p4 = add_mate(4, c4)
    c6 = begin(6)
    p5 = add_mate(5, c5)
    q3 = pass_on(3, p3)
    p6 = add_mate(6, c6)
    offset.wait_recv()
    spread_rows(offin, 1024)
    to_z(2, q2)
    q4 = pass_on(4, p4)
    to_z(3, q3)
    q5 = pass_on(5, p5)
    q6 = pass_on(6, p6)
    diag = jnp.concatenate([from_z(0), from_z(1)], axis=1) / 65536.0
    to_z(4, q4)
    to_z(5, q5)
    to_z(6, q6)
    cross0 = from_z(2)
    cross1 = from_z(3)
    strip[0] = from_z(4)
    hop0 = keep(send(strip.at[0], hop.at[0], s_h.at[0], r_h.at[0], pair))
    strip[1] = from_z(5)
    hop1 = keep(send(strip.at[1], hop.at[1], s_h.at[1], r_h.at[1], pair))
    cross2 = from_z(6)
    hop0.wait_recv()
    hop1.wait_recv()
    cross = jnp.concatenate([cross0, cross1, cross2], axis=1)
    cross = (cross + jnp.concatenate([hop[0], hop[1]], axis=1)) / 65536.0
    cov_ref[:, :1024] = jnp.where(parity == 0, diag, cross)
    cov_ref[:, 1024:] = jnp.where(parity == 0, cross, diag)
    for copy in out:
        copy.wait_send()


def whole(q, k, v, log_decay, gain):
    count, width = q.shape
    vm = pl.BlockSpec(memory_space=pltpu.VMEM)
    hbm = pl.BlockSpec(memory_space=pl.ANY)
    dma = pltpu.SemaphoreType.DMA

    def f32(*shape):
        return pltpu.VMEM(shape, F32)

    def bf16(*shape):
        return pltpu.VMEM(shape, BF16)

    def per_segment(*shape, share=1):
        return tuple(pltpu.VMEM((*shape, wide // share), BF16) for _, _, wide in SEGMENTS)

    return pl.pallas_call(
        kernel,
        out_shape=(
            jax.ShapeDtypeStruct((8, D), F32),
            jax.ShapeDtypeStruct((16, 2048), F32),
        ),
        in_specs=[hbm, hbm, hbm, vm, vm],
        out_specs=(vm, vm),
        scratch_shapes=[
            bf16(count, width),
            bf16(count, width),
            bf16(count, width),
            bf16(count, width),
            f32(24, D),
            f32(8, 1024),
            f32(8, 1024, D),
            f32(8, 1024, D),
            f32(8, 4, D, D),
            f32(2, 2, NZ, PIECE + 8, D),
            f32(2, NZ, PIECE + 8, D),
            f32(2, NZ, PIECE + 8, D),
            f32(2, NZ, PIECE + 8, D),
            f32(2, NZ, PIECE + 8, D),
            f32(2, NY, PIECE + 8, D),
            f32(2, NZ, PIECE, D),
            f32(2, NZ, PIECE, D),
            f32(2, NZ, PIECE, D),
            f32(2, 2, NZ, PIECE, D),
            bf16(512, 1024),
            f32(2, 16, 512),
            f32(2, 16, 512),
            f32(NY, 2, 8, D),
            f32(24, D),
            f32(NZ, 24, D),
            f32(NY, 24, D),
            f32(2 * NY, 8, D),
            f32(2 * NY, 8, D),
            bf16(32, 2048),
            bf16(32, 2048),
            per_segment(32, 2, 16),
            per_segment(32, 16),
            per_segment(32, 16),
            per_segment(NZ, 16, share=2),
            per_segment(NZ, 16, share=2),
            per_segment(NZ, 16),
            per_segment(NZ, 16),
            per_segment(NZ, 16),
            per_segment(NZ, 16),
            per_segment(NZ, 16),
            per_segment(NZ, 16),
            dma((5,)), dma((2,)), dma((2,)), dma((2, NZ)), dma((2, NZ)), dma((2, NY)), dma((2, NY)),
            dma((2, NZ)), dma((2, NZ)), dma((2,)), dma((2,)),
            dma, dma, dma((4,)), dma((4,)), dma((SEGS,)), dma((SEGS,)),
            dma((SEGS, 2)), dma((SEGS, 2)), dma((SEGS, 2)), dma((SEGS, 2)),
            dma((SEGS, NZ)), dma((SEGS, NZ)), dma((2,)), dma((2,)),
            dma, dma, dma((NZ,)), dma((NZ,)), dma((NY,)), dma((NY,)), dma((NY,)), dma((NY,)),
        ],
        compiler_params=pltpu.CompilerParams(
            collective_id=0, has_side_effects=True, vmem_limit_bytes=60 * 1024 * 1024
        ),
        name="whole",
    )(q, k, v, log_decay, gain.reshape(8, D))


def hand_kernel(a_ref, b_ref, c_ref, d_ref):
    c_ref[...] = a_ref[...]
    d_ref[...] = b_ref[...]


def hand_out(shift, covariance):
    vm = pl.BlockSpec(memory_space=pltpu.VMEM)
    return pl.pallas_call(
        hand_kernel,
        out_shape=(
            jax.ShapeDtypeStruct(shift.shape, F32),
            jax.ShapeDtypeStruct(covariance.shape, F32),
        ),
        in_specs=[vm] * 2,
        out_specs=(vm, vm),
        name="hand_out",
    )(shift, covariance)


def body(queries, keys, values, log_decay, gain):
    shift, covariance = hand_out(*whole(queries, keys, values, log_decay, gain))
    return (shift.reshape(-1), covariance)


def solution(mesh):
    placed = (P("ctx", "head"), P("ctx", "head"), P("ctx", "head"), P("head", "ctx"), P("head"))
    return jax.shard_map(
        body,
        mesh=mesh,
        in_specs=placed,
        out_specs=(P("head"), P(("head", "ctx"), None)),
        check_vma=False,
    )
```

```python
import functools

import jax
import jax.numpy as jnp
from jax import lax
from jax.experimental import pallas as pl
from jax.experimental.pallas import tpu as pltpu
from jax.sharding import PartitionSpec as P

D = 128
SPAN = 256
NZ = 8
NY = 4
F32 = jnp.float32
BF16 = jnp.bfloat16
MESH = pl.DeviceIdType.MESH
TOK = (((0,), (0,)), ((), ()))
LAST = (((1,), (1,)), ((), ()))


def place():
    me = lax.axis_index("ctx")
    core = lax.rem(me, 2)
    z = lax.rem(me // 2, NZ)
    y = me // (2 * NZ)
    return y, z, core


def at(y, z, core):
    return {"ctx": (y * NZ + z) * 2 + core}


def greet(peers):
    barrier = pltpu.get_barrier_semaphore()
    for peer in peers:
        pl.semaphore_signal(barrier, inc=1, device_id=peer, device_id_type=MESH)
    return lambda: pl.semaphore_wait(barrier, len(peers))


def send(src, dst, ssem, rsem, peer):
    copy = pltpu.make_async_remote_copy(
        src_ref=src, dst_ref=dst, send_sem=ssem, recv_sem=rsem, device_id=peer, device_id_type=MESH
    )
    copy.start()
    return copy


def arrived(src, dst, ssem, rsem, peer):
    pltpu.make_async_remote_copy(
        src_ref=src, dst_ref=dst, send_sem=ssem, recv_sem=rsem, device_id=peer, device_id_type=MESH
    ).wait_recv()


def plane_peers(y, z, core):
    peers = [at(y, z, 1 - core)]
    peers += [at(y, lax.rem(z + i, NZ), core) for i in range(1, NZ)]
    peers += [at(lax.rem(y + i, NY), z, core) for i in range(1, NY)]
    return peers


PIECE = 32
DIAG, CROSS, TURNED = 0, 1, 2
SEGMENTS = (
    (DIAG, 0, 512),
    (DIAG, 512, 512),
    (CROSS, 0, 512),
    (CROSS, 512, 256),
    (TURNED, 0, 512),
    (TURNED, 512, 512),
    (CROSS, 768, 256),
)
SEGS = len(SEGMENTS)


def expand(piece):
    return jnp.concatenate(
        [jnp.broadcast_to(piece[PIECE + i : PIECE + i + 1], (16, D)) for i in range(2)], axis=0
    )


def join(first, second):
    return expand(second) * first[:PIECE] + second[:PIECE], first[PIECE:] * second[PIECE:]


def kernel(
    q_hbm, k_hbm, v_hbm, ld_ref, gain_ref, shift_hbm, cov_hbm,
    q_ref, k_ref, v_ref, c_ref, st_ref,
    cum, col, inner, upd, part, other, chip, zin, pre, yin, back, chipin, give, sin,
    theirs, shift_ref, diag_ref, cross_ref, means, armate, stz, sty, off, offin, left, right,
    grams, mates, sums, ylow, yhigh, yfirst, ylast, ynext, yprev, zsend, zgot,
    s_in, s_core, r_core, s_z, r_z, s_y, r_y, s_zb, r_zb, s_cb, r_cb,
    s_m, r_m, s_x, r_x, s_c, r_c, s_y1, r_y1, s_y2, r_y2, s_zz, r_zz, s_out,
    s_s1, r_s1, s_sz, r_sz, s_sy, r_sy, s_g, r_g,
):
    y, z, core = place()
    parity = lax.rem(lax.axis_index("head"), 2)
    pair = {"head": lax.axis_index("head") + 1 - 2 * parity}
    mate = at(y, z, 1 - core)
    north, south = lax.rem(y + 1, NY), lax.rem(y + NY - 1, NY)
    far = lax.rem(y + 2, NY)
    beyond = lax.axis_index("head") + 1 - 2 * parity

    def across(to):
        return {**at(y, to, core), "head": beyond}

    ready = greet(
        plane_peers(y, z, core) + [across(lax.rem(z + i, NZ)) for i in range(NZ)]
    )
    out = []

    def keep(copy):
        out.append(copy)
        return copy

    def batch(ref, sem):
        return pltpu.make_async_remote_copy(
            src_ref=ref, dst_ref=ref, send_sem=sem, recv_sem=sem, device_id=mate, device_id_type=MESH
        )

    def load(src, dst, sem):
        copy = pltpu.make_async_copy(src, dst, sem)
        copy.start()
        return copy

    def half_of(ref, g):
        return ref.at[:, pl.ds(g * 512, 512)]

    kv_in = [
        (
            load(half_of(k_hbm, g), half_of(k_ref, g), s_in.at[2 * g]),
            load(half_of(v_hbm, g), half_of(v_ref, g), s_in.at[2 * g + 1]),
        )
        for g in range(2)
    ]
    q_in = load(q_hbm, q_ref, s_in.at[4])

    total = ld_ref[...]
    lane = lax.rem(lax.broadcasted_iota(jnp.int32, total.shape, 1), SPAN)
    step = 1
    while step < SPAN:
        total = total + jnp.where(lane >= step, pltpu.roll(total, step, 1), 0.0)
        step *= 2
    cum[...] = total
    turned = jnp.transpose(total)

    def columns_of(heads):
        for head in heads:
            col[head] = jnp.broadcast_to(turned[:, head : head + 1], (4 * SPAN, D))

    columns_of(range(4))
    part[...] = jnp.zeros_like(part)

    def lanes(head):
        return pl.ds(pl.multiple_of(head * D, D), D)

    def both_heads(work):
        def turn(i, carry):
            work(i)
            return carry

        lax.fori_loop(0, 2, turn, 0)

    def update(g, owning):
        def one(i):
            head = 4 * g + 2 * owning + i
            ending = jnp.zeros((D, D), F32)
            decay = jnp.zeros((1, D), F32)
            for b in range(4):
                rows = pl.ds(b * SPAN, SPAN)
                last = col[head, pl.ds(b * SPAN + SPAN - 1, 1), :]
                scaled = v_ref[rows, lanes(head)].astype(F32) * jnp.exp(last - col[head, rows, :])
                high = scaled.astype(BF16)
                low = (scaled - high.astype(F32)).astype(BF16)
                both = lax.dot_general(
                    k_ref[rows, lanes(head)],
                    jnp.concatenate([high, low], axis=1),
                    TOK,
                    preferred_element_type=F32,
                )
                new = both[:, :D] + both[:, D:]
                upd[head, b] = new
                ending = jnp.exp(last) * ending + new
                decay = decay + last
            for owner in range(NZ):
                part[g, owning, owner, pl.ds(pl.multiple_of(i * 16, 16), 16), :] = ending[
                    owner * 16 : owner * 16 + 16
                ]
                part[g, owning, owner, pl.ds(PIECE + i, 1), :] = jnp.exp(decay)

        both_heads(one)

    later = lax.broadcasted_iota(jnp.int32, (SPAN, SPAN), 0) >= lax.broadcasted_iota(
        jnp.int32, (SPAN, SPAN), 1
    )

    def within(lo, hi):
        def turn(head, carry):
            for b in range(4):
                rows = pl.ds(b * SPAN, SPAN)
                scores = lax.dot_general(
                    q_ref[rows, lanes(head)],
                    k_ref[rows, lanes(head)],
                    LAST,
                    preferred_element_type=F32,
                )
                mine = col[head, rows, :]
                diff = jnp.concatenate([mine, mine], axis=1) - cum[pl.ds(head, 1), rows]
                weights = jnp.where(later, scores * jnp.exp(jnp.minimum(diff, 0.0)), 0.0)
                inner[head, rows, :] = jnp.dot(
                    weights.astype(BF16), v_ref[rows, lanes(head)], preferred_element_type=F32
                )
            return carry

        lax.fori_loop(lo, hi, turn, 0)

    def to_core(g):
        return keep(send(part.at[g, 1 - core], other.at[g], s_core.at[g], r_core.at[g], mate))

    def to_owners(g, copy):
        copy.wait_recv()

        def combine(owner, carry):
            mine, theirs_ = part[g, core, owner], other[g, owner]
            first = jnp.where(core == 0, mine, theirs_)
            second = jnp.where(core == 0, theirs_, mine)
            state, decay = join(first, second)
            chip[g, owner, :PIECE, :] = state
            chip[g, owner, PIECE:, :] = decay
            return carry

        lax.fori_loop(0, NZ, combine, 0)
        for i in range(1, NZ):
            to = lax.rem(z + i, NZ)
            send(chip.at[g, to], zin.at[g, z], s_z.at[g], r_z.at[g], at(y, to, core))
        keep(batch(chip.at[g, pl.ds(0, NZ - 1)], s_z.at[g]))
        zin[g, z] = chip[g, z]

    def to_rows(g):
        batch(zin.at[g, pl.ds(0, NZ - 1)], r_z.at[g]).wait_recv()
        state, decay = jnp.zeros((PIECE, D), F32), jnp.ones((8, D), F32)
        for j in range(NZ):
            pre[g, j, :PIECE, :] = state
            pre[g, j, PIECE:, :] = decay
            state, decay = join(jnp.concatenate([state, decay], axis=0), zin[g, j])
        yin[g, y, :PIECE, :] = state
        yin[g, y, PIECE:, :] = decay
        for i in range(1, NY):
            to = lax.rem(y + i, NY)
            send(yin.at[g, y], yin.at[g, y], s_y.at[g], r_y.at[g], at(to, z, core))
        keep(batch(yin.at[g, pl.ds(0, NY - 1)], s_y.at[g]))

    def to_chips(g):
        batch(yin.at[g, pl.ds(0, NY - 1)], r_y.at[g]).wait_recv()
        row = jnp.zeros((PIECE, D), F32)
        for j in range(NY):
            piece = yin[g, j]
            row = jnp.where(j < y, expand(piece) * row + piece[:PIECE], row)
        for j in range(NZ):
            piece = pre[g, j]
            back[g, j] = expand(piece) * row + piece[:PIECE]
        for i in range(1, NZ):
            to = lax.rem(z + i, NZ)
            send(back.at[g, to], chipin.at[g, z], s_zb.at[g], r_zb.at[g], at(y, to, core))
        keep(batch(back.at[g, pl.ds(0, NZ - 1)], s_zb.at[g]))
        chipin[g, z] = back[g, z]

    def to_cores(g):
        batch(chipin.at[g, pl.ds(0, NZ - 1)], r_zb.at[g]).wait_recv()

        def split(owner, carry):
            lead = jnp.where(core == 0, part[g, core, owner], other[g, owner])
            early = chipin[g, owner]
            late = expand(lead) * early + lead[:PIECE]
            give[g, owner] = jnp.where(core == 0, late, early)
            sin[g, core, owner] = jnp.where(core == 0, early, late)
            return carry

        lax.fori_loop(0, NZ, split, 0)
        return keep(send(give.at[g], sin.at[g, core], s_cb.at[g], r_cb.at[g], mate))

    def finish(g, owning):
        def one(i):
            head = 4 * g + 2 * owning + i
            state = jnp.concatenate(
                [
                    sin[g, owning, owner, pl.ds(pl.multiple_of(i * 16, 16), 16), :]
                    for owner in range(NZ)
                ],
                axis=0,
            )
            gain = gain_ref[pl.ds(head, 1), :]
            mean = jnp.zeros((1, D), F32)
            top = bottom = None
            for b in range(4):
                rows = pl.ds(b * SPAN, SPAN)
                high = state.astype(BF16)
                low = (state - high.astype(F32)).astype(BF16)
                both = jnp.dot(
                    q_ref[rows, lanes(head)],
                    jnp.concatenate([high, low], axis=1),
                    preferred_element_type=F32,
                )
                raw = inner[head, rows, :] + jnp.exp(col[head, rows, :]) * (both[:, :D] + both[:, D:])
                scale = jnp.sqrt(jnp.mean(raw * raw, axis=1, keepdims=True) + 1e-06)
                done = (raw / scale * gain).astype(BF16).astype(F32)
                mean = mean + jnp.sum(done, axis=0, keepdims=True)
                high_b = jnp.max(done, axis=0, keepdims=True)
                low_b = jnp.min(done, axis=0, keepdims=True)
                top = high_b if top is None else jnp.maximum(top, high_b)
                bottom = low_b if bottom is None else jnp.minimum(bottom, low_b)
                inner[head, rows, :] = done
                if b < 3:
                    last = col[head, pl.ds(b * SPAN + SPAN - 1, 1), :]
                    state = jnp.exp(last) * state + upd[head, b]
            mean = mean / (4 * SPAN)
            for b in range(4):
                rows = pl.ds(b * SPAN, SPAN)
                c_ref[rows, lanes(head)] = (inner[head, rows, :] - mean).astype(BF16)
            st_ref[pl.ds(head, 1), :] = mean
            st_ref[pl.ds(8 + head, 1), :] = top
            st_ref[pl.ds(16 + head, 1), :] = bottom

        both_heads(one)

    other_half = pl.ds(pl.multiple_of((1 - parity) * 512, 512), 512)
    half = pl.ds(pl.multiple_of(parity * 512, 512), 512)

    def columns(j):
        return pl.ds(pl.multiple_of(j * 256, 256), 256)

    def to_pair(j):
        return keep(
            send(
                c_ref.at[other_half, columns(j)],
                theirs.at[:, columns(j)],
                s_x.at[j],
                r_x.at[j],
                pair,
            )
        )

    def from_pair(j):
        arrived(
            c_ref.at[other_half, columns(j)], theirs.at[:, columns(j)], s_x.at[j], r_x.at[j], pair
        )

    targets = (far, north, south, y)

    def begin(seg):
        kind, first, wide = SEGMENTS[seg]
        cols = slice(first, first + wide)
        copies = []
        for i, target in enumerate(targets):
            rows = columns(target)
            if kind == DIAG:
                a, b = c_ref[:, rows], c_ref[:, cols]
            elif kind == CROSS:
                a, b = c_ref[half, rows], theirs[:, cols]
            else:
                a, b = theirs[:, rows], c_ref[half, cols]
            value = lax.dot_general(a, b, TOK, preferred_element_type=F32)
            grams[seg][i] = value.astype(BF16).reshape(NZ, 2, 16, wide)
            if i in (0, 3):
                span = pl.ds(0, 1) if i == 0 else pl.ds(1, 3)
                copies.append(
                    send(
                        grams[seg].at[span, :, 1 - core],
                        mates[seg].at[span],
                        s_c.at[seg],
                        r_c.at[seg, i // 3],
                        mate,
                    )
                )
        keep(batch(mates[seg], s_c.at[seg]))
        return copies

    def chip_sum(seg, i, which):
        return grams[seg][i, which, core].astype(F32) + mates[seg][i, which].astype(F32)

    def merge(a, b):
        return jnp.concatenate(
            [a[:8] + b[:8], jnp.maximum(a[8:16], b[8:16]), jnp.minimum(a[16:], b[16:])], axis=0
        )

    def add_mate(seg, copies):
        copies[0].wait_recv()

        def turn(i, carry):
            two = pl.ds(i * 2, 2)
            sums[seg][two] = chip_sum(seg, 0, two).astype(BF16)
            return carry

        lax.fori_loop(0, 4, turn, 0)
        edge = SEGMENTS[seg][2] // 2
        send(sums[seg].at[:, :, pl.ds(0, edge)], ylow[seg], s_y1.at[seg], r_y1.at[seg], at(north, z, core))
        send(sums[seg].at[:, :, pl.ds(edge, edge)], yhigh[seg], s_y1.at[seg], r_y1.at[seg], at(south, z, core))
        keep(batch(sums[seg], s_y1.at[seg]))
        return copies[1]

    def pass_on(seg, rest):
        batch(sums[seg], r_y1.at[seg]).wait_recv()
        rest.wait_recv()
        edge = SEGMENTS[seg][2] // 2

        def turn(i, carry):
            two = pl.ds(i * 2, 2)
            a = chip_sum(seg, 1, two)
            b = chip_sum(seg, 2, two)
            low = a[:, :, :edge] + ylow[seg][two].astype(F32)
            high = b[:, :, edge:] + yhigh[seg][two].astype(F32)
            ynext[seg][two, :, :edge] = low.astype(BF16)
            ynext[seg][two, :, edge:] = a[:, :, edge:].astype(BF16)
            yprev[seg][two, :, :edge] = b[:, :, :edge].astype(BF16)
            yprev[seg][two, :, edge:] = high.astype(BF16)
            return carry

        lax.fori_loop(0, 4, turn, 0)
        send(ynext[seg], yfirst[seg], s_y2.at[seg], r_y2.at[seg], at(north, z, core))
        send(yprev[seg], ylast[seg], s_y2.at[seg], r_y2.at[seg], at(south, z, core))
        keep(batch(mates[seg].at[pl.ds(0, 2)], s_y2.at[seg]))

    def to_z(seg):
        batch(mates[seg].at[pl.ds(0, 2)], r_y2.at[seg]).wait_recv()
        kind, first, wide = SEGMENTS[seg]
        tall = 1024 if kind == TURNED else 0
        start = first + (1024 if kind == CROSS else 0)
        spread = lax.dot_general(
            left[:, pl.ds(pl.multiple_of(tall + y * 256, 256), 256)],
            right[:, start : start + wide],
            TOK,
            preferred_element_type=F32,
        )
        spread = spread.reshape(NZ, 2, 16, wide) * (1024.0 if kind == DIAG else 512.0)
        spread = jnp.where(core == 0, spread[:, 0], spread[:, 1])
        got = chip_sum(seg, 3, pl.ds(0, NZ)) + yfirst[seg][...].astype(F32)
        got = got + ylast[seg][...].astype(F32) + spread
        zsend[seg][...] = got.astype(BF16)
        for i in range(0 if kind == TURNED else 1, NZ):
            to = lax.rem(z + i, NZ)
            peer = across(to) if kind == TURNED else at(y, to, core)
            send(zsend[seg].at[to], zgot[seg].at[z], s_zz.at[seg], r_zz.at[seg], peer)
        count = NZ if kind == TURNED else NZ - 1
        keep(batch(zsend[seg].at[pl.ds(0, count)], s_zz.at[seg]))
        if kind != TURNED:
            zgot[seg][z] = zsend[seg][z]

    def from_z(seg):
        count = NZ if SEGMENTS[seg][0] == TURNED else NZ - 1
        batch(zgot[seg].at[pl.ds(0, count)], r_zz.at[seg]).wait_recv()
        got = zgot[seg][0].astype(F32)
        for j in range(1, NZ):
            got = got + zgot[seg][j].astype(F32)
        return got

    def kv_ready(g):
        kv_in[g][0].wait()
        kv_in[g][1].wait()

    kv_ready(0)
    update(0, 1 - core)
    ready()
    b0 = to_core(0)
    update(0, core)
    columns_of(range(4, 8))
    kv_ready(1)
    update(1, 1 - core)
    b1 = to_core(1)
    to_owners(0, b0)
    update(1, core)
    to_owners(1, b1)
    q_in.wait()
    within(0, 6)
    to_rows(0)
    within(6, 7)
    to_rows(1)
    within(7, 8)
    to_chips(0)
    to_chips(1)
    e0 = to_cores(0)
    finish(0, core)
    to_pair(core)
    e0.wait_recv()
    finish(0, 1 - core)
    to_pair(1 - core)
    e1 = to_cores(1)
    finish(1, core)
    e1.wait_recv()
    finish(1, 1 - core)
    first = keep(send(st_ref, armate, s_s1, r_s1, mate))
    to_pair(2)
    to_pair(3)
    means[y, core] = st_ref[:8, :]

    def spread_rows(source, base):
        for j in range(8):
            piece = source[:, j, :]
            high = piece.astype(BF16)
            low = (piece - high.astype(F32)).astype(BF16)
            none = jnp.zeros_like(high)
            cols = slice(base + j * D, base + j * D + D)
            left[:, cols] = jnp.concatenate([high, high, low, none], axis=0)
            right[:, cols] = jnp.concatenate([high, low, high, none], axis=0)

    c0 = begin(0)
    first.wait_recv()
    means[y, 1 - core] = armate[:8, :]
    stz[z] = merge(st_ref[...], armate[...])
    for i in range(1, NZ):
        to = lax.rem(z + i, NZ)
        send(stz.at[z], stz.at[z], s_sz, r_sz, at(y, to, core))
    keep(batch(stz.at[pl.ds(0, NZ - 1)], s_sz))
    for i in range(1, NY):
        to = lax.rem(y + i, NY)
        send(means.at[y], means.at[y], s_g, r_g, at(to, z, core))
    keep(batch(means.at[pl.ds(0, NY - 1)], s_g))
    c1 = begin(1)
    p0 = add_mate(0, c0)
    p1 = add_mate(1, c1)
    pass_on(0, p0)
    from_pair(core)
    from_pair(1 - core)
    c2 = begin(2)
    pass_on(1, p1)
    batch(stz.at[pl.ds(0, NZ - 1)], r_sz).wait_recv()
    sty[y] = functools.reduce(merge, [stz[j] for j in range(NZ)])
    for i in range(1, NY):
        to = lax.rem(y + i, NY)
        send(sty.at[y], sty.at[y], s_sy, r_sy, at(to, z, core))
    keep(batch(sty.at[pl.ds(0, NY - 1)], s_sy))
    p2 = add_mate(2, c2)
    from_pair(2)
    c3 = begin(3)
    batch(means.at[pl.ds(0, NY - 1)], r_g).wait_recv()
    batch(sty.at[pl.ds(0, NY - 1)], r_sy).wait_recv()
    every = functools.reduce(merge, [sty[j] for j in range(NY)])
    shift_ref[...] = (every[8:16] + every[16:]) / 2.0
    writes = [load(shift_ref, shift_hbm, s_out.at[0])]
    off[...] = means[...].reshape(NY * 2, 8, D) - (every[:8] / 64.0)[None]
    offset = keep(send(off, offin, s_m, r_m, pair))
    spread_rows(off, 0)
    to_z(0)
    to_z(1)
    pass_on(2, p2)
    p3 = add_mate(3, c3)
    from_pair(3)
    c4 = begin(4)
    c5 = begin(5)
    p4 = add_mate(4, c4)
    c6 = begin(6)
    p5 = add_mate(5, c5)
    pass_on(3, p3)
    p6 = add_mate(6, c6)
    offset.wait_recv()
    spread_rows(offin, 1024)
    to_z(2)
    pass_on(4, p4)
    to_z(3)
    pass_on(5, p5)
    pass_on(6, p6)
    diag_ref[...] = jnp.concatenate([from_z(0), from_z(1)], axis=1) / 65536.0
    block = pl.ds(pl.multiple_of(parity * 1024, 1024), 1024)
    writes.append(load(diag_ref, cov_hbm.at[:, block], s_out.at[1]))
    to_z(4)
    to_z(5)
    to_z(6)
    cross_ref[:, :512] = from_z(2)
    cross_ref[:, 512:768] = from_z(3)
    cross_ref[:, :512] = (cross_ref[:, :512] + from_z(4)) / 65536.0
    turned1 = from_z(5)
    cross_ref[:, 512:768] = (cross_ref[:, 512:768] + turned1[:, :256]) / 65536.0
    cross_ref[:, 768:] = (from_z(6) + turned1[:, 256:]) / 65536.0
    block = pl.ds(pl.multiple_of((1 - parity) * 1024, 1024), 1024)
    writes.append(load(cross_ref, cov_hbm.at[:, block], s_out.at[2]))
    for copy in writes:
        copy.wait()
    for copy in out:
        copy.wait_send()


def whole(q, k, v, log_decay, gain):
    count, width = q.shape
    vm = pl.BlockSpec(memory_space=pltpu.VMEM)
    hbm = pl.BlockSpec(memory_space=pl.ANY)
    dma = pltpu.SemaphoreType.DMA

    def f32(*shape):
        return pltpu.VMEM(shape, F32)

    def bf16(*shape):
        return pltpu.VMEM(shape, BF16)

    def per_segment(*shape, share=1):
        return tuple(pltpu.VMEM((*shape, wide // share), BF16) for _, _, wide in SEGMENTS)

    return pl.pallas_call(
        kernel,
        out_shape=(
            jax.ShapeDtypeStruct((8, D), F32),
            jax.ShapeDtypeStruct((16, 2048), F32),
        ),
        in_specs=[hbm, hbm, hbm, vm, vm],
        out_specs=(hbm, hbm),
        scratch_shapes=[
            bf16(count, width),
            bf16(count, width),
            bf16(count, width),
            bf16(count, width),
            f32(24, D),
            f32(8, 1024),
            f32(8, 1024, D),
            f32(8, 1024, D),
            f32(8, 4, D, D),
            f32(2, 2, NZ, PIECE + 8, D),
            f32(2, NZ, PIECE + 8, D),
            f32(2, NZ, PIECE + 8, D),
            f32(2, NZ, PIECE + 8, D),
            f32(2, NZ, PIECE + 8, D),
            f32(2, NY, PIECE + 8, D),
            f32(2, NZ, PIECE, D),
            f32(2, NZ, PIECE, D),
            f32(2, NZ, PIECE, D),
            f32(2, 2, NZ, PIECE, D),
            bf16(512, 1024),
            f32(8, D),
            f32(16, 1024),
            f32(16, 1024),
            f32(NY, 2, 8, D),
            f32(24, D),
            f32(NZ, 24, D),
            f32(NY, 24, D),
            f32(2 * NY, 8, D),
            f32(2 * NY, 8, D),
            bf16(32, 2048),
            bf16(32, 2048),
            per_segment(NY, NZ, 2, 16),
            per_segment(NY, NZ, 16),
            per_segment(NZ, 16),
            per_segment(NZ, 16, share=2),
            per_segment(NZ, 16, share=2),
            per_segment(NZ, 16),
            per_segment(NZ, 16),
            per_segment(NZ, 16),
            per_segment(NZ, 16),
            per_segment(NZ, 16),
            per_segment(NZ, 16),
            dma((5,)), dma((2,)), dma((2,)), dma((2,)), dma((2,)), dma((2,)), dma((2,)),
            dma((2,)), dma((2,)), dma((2,)), dma((2,)),
            dma, dma, dma((4,)), dma((4,)), dma((SEGS,)), dma((SEGS, 2)),
            dma((SEGS,)), dma((SEGS,)), dma((SEGS,)), dma((SEGS,)), dma((SEGS,)), dma((SEGS,)), dma((3,)),
            dma, dma, dma, dma, dma, dma, dma, dma,
        ],
        compiler_params=pltpu.CompilerParams(
            collective_id=0, has_side_effects=True, vmem_limit_bytes=60 * 1024 * 1024
        ),
        name="whole",
    )(q, k, v, log_decay, gain.reshape(8, D))


def hand_kernel(a_ref, b_ref, c_ref, d_ref):
    c_ref[...] = a_ref[...]
    d_ref[...] = b_ref[...]


def hand_out(shift, covariance):
    vm = pl.BlockSpec(memory_space=pltpu.VMEM)
    return pl.pallas_call(
        hand_kernel,
        out_shape=(
            jax.ShapeDtypeStruct(shift.shape, F32),
            jax.ShapeDtypeStruct(covariance.shape, F32),
        ),
        in_specs=[vm] * 2,
        out_specs=(vm, vm),
        name="hand_out",
    )(shift, covariance)


def body(queries, keys, values, log_decay, gain):
    shift, covariance = hand_out(*whole(queries, keys, values, log_decay, gain))
    return (shift.reshape(-1), covariance)


def solution(mesh):
    placed = (P("ctx", "head"), P("ctx", "head"), P("ctx", "head"), P("head", "ctx"), P("head"))
    return jax.shard_map(
        body,
        mesh=mesh,
        in_specs=placed,
        out_specs=(P("head"), P(("head", "ctx"), None)),
        check_vma=False,
    )
```

```python
import functools

import jax
import jax.numpy as jnp
from jax import lax
from jax.experimental import pallas as pl
from jax.experimental.pallas import tpu as pltpu
from jax.sharding import PartitionSpec as P

D = 128
SPAN = 256
NZ = 8
NY = 4
F32 = jnp.float32
BF16 = jnp.bfloat16
MESH = pl.DeviceIdType.MESH
TOK = (((0,), (0,)), ((), ()))
LAST = (((1,), (1,)), ((), ()))


def place():
    me = lax.axis_index("ctx")
    core = lax.rem(me, 2)
    z = lax.rem(me // 2, NZ)
    y = me // (2 * NZ)
    return y, z, core


def at(y, z, core):
    return {"ctx": (y * NZ + z) * 2 + core}


def greet(peers):
    barrier = pltpu.get_barrier_semaphore()
    for peer in peers:
        pl.semaphore_signal(barrier, inc=1, device_id=peer, device_id_type=MESH)
    return lambda: pl.semaphore_wait(barrier, len(peers))


def send(src, dst, ssem, rsem, peer):
    copy = pltpu.make_async_remote_copy(
        src_ref=src, dst_ref=dst, send_sem=ssem, recv_sem=rsem, device_id=peer, device_id_type=MESH
    )
    copy.start()
    return copy


def arrived(src, dst, ssem, rsem, peer):
    pltpu.make_async_remote_copy(
        src_ref=src, dst_ref=dst, send_sem=ssem, recv_sem=rsem, device_id=peer, device_id_type=MESH
    ).wait_recv()


def plane_peers(y, z, core):
    peers = [at(y, z, 1 - core)]
    peers += [at(y, lax.rem(z + i, NZ), core) for i in range(1, NZ)]
    peers += [at(lax.rem(y + i, NY), z, core) for i in range(1, NY)]
    return peers


PIECE = 32
DIAG, CROSS, TURNED = 0, 1, 2
SEGMENTS = (
    (DIAG, 0, 512),
    (DIAG, 512, 512),
    (CROSS, 0, 512),
    (CROSS, 512, 256),
    (TURNED, 0, 512),
    (TURNED, 512, 512),
    (CROSS, 768, 256),
)
SEGS = len(SEGMENTS)


def expand(piece):
    return jnp.concatenate(
        [jnp.broadcast_to(piece[PIECE + i : PIECE + i + 1], (16, D)) for i in range(2)], axis=0
    )


def join(first, second):
    return expand(second) * first[:PIECE] + second[:PIECE], first[PIECE:] * second[PIECE:]


def kernel(
    q_hbm, k_hbm, v_hbm, ld_ref, gain_ref, shift_hbm, cov_hbm,
    q_ref, k_ref, v_ref, c_ref, st_ref,
    cum, col, inner, upd, part, other, chip, zin, pre, yin, back, chipin, give, sin,
    theirs, shift_ref, diag_ref, cross_ref, means, armate, stz, sty, off, offin, left, right,
    grams, mates, sums, ylow, yhigh, yfirst, ylast, ynext, yprev, zsend, zgot,
    s_in, s_core, r_core, s_z, r_z, s_y, r_y, s_zb, r_zb, s_cb, r_cb,
    s_m, r_m, s_x, r_x, s_c, r_c, s_y1, r_y1, s_y2, r_y2, s_zz, r_zz, s_out,
    s_s1, r_s1, s_sz, r_sz, s_sy, r_sy, s_g, r_g,
):
    y, z, core = place()
    parity = lax.rem(lax.axis_index("head"), 2)
    pair = {"head": lax.axis_index("head") + 1 - 2 * parity}
    mate = at(y, z, 1 - core)
    north, south = lax.rem(y + 1, NY), lax.rem(y + NY - 1, NY)
    far = lax.rem(y + 2, NY)
    beyond = lax.axis_index("head") + 1 - 2 * parity

    def across(to):
        return {**at(y, to, core), "head": beyond}

    ready = greet(
        plane_peers(y, z, core) + [across(lax.rem(z + i, NZ)) for i in range(NZ)]
    )
    out = []

    def keep(copy):
        out.append(copy)
        return copy

    def batch(ref, sem):
        return pltpu.make_async_remote_copy(
            src_ref=ref, dst_ref=ref, send_sem=sem, recv_sem=sem, device_id=mate, device_id_type=MESH
        )

    def load(src, dst, sem):
        copy = pltpu.make_async_copy(src, dst, sem)
        copy.start()
        return copy

    def half_of(ref, g):
        return ref.at[:, pl.ds(g * 512, 512)]

    kv_in = [
        (
            load(half_of(k_hbm, g), half_of(k_ref, g), s_in.at[2 * g]),
            load(half_of(v_hbm, g), half_of(v_ref, g), s_in.at[2 * g + 1]),
        )
        for g in range(2)
    ]
    q_in = load(q_hbm, q_ref, s_in.at[4])

    total = ld_ref[...]
    lane = lax.rem(lax.broadcasted_iota(jnp.int32, total.shape, 1), SPAN)
    step = 1
    while step < SPAN:
        total = total + jnp.where(lane >= step, pltpu.roll(total, step, 1), 0.0)
        step *= 2
    cum[...] = total
    turned = jnp.transpose(total)

    def columns_of(heads):
        for head in heads:
            col[head] = jnp.broadcast_to(turned[:, head : head + 1], (4 * SPAN, D))

    columns_of(range(4))
    part[...] = jnp.zeros_like(part)

    def lanes(head):
        return pl.ds(pl.multiple_of(head * D, D), D)

    def both_heads(work):
        def turn(i, carry):
            work(i)
            return carry

        lax.fori_loop(0, 2, turn, 0)

    def update(g, owning):
        def one(i):
            head = 4 * g + 2 * owning + i
            ending = jnp.zeros((D, D), F32)
            decay = jnp.zeros((1, D), F32)
            for b in range(4):
                rows = pl.ds(b * SPAN, SPAN)
                last = col[head, pl.ds(b * SPAN + SPAN - 1, 1), :]
                scaled = v_ref[rows, lanes(head)].astype(F32) * jnp.exp(last - col[head, rows, :])
                high = scaled.astype(BF16)
                low = (scaled - high.astype(F32)).astype(BF16)
                both = lax.dot_general(
                    k_ref[rows, lanes(head)],
                    jnp.concatenate([high, low], axis=1),
                    TOK,
                    preferred_element_type=F32,
                )
                new = both[:, :D] + both[:, D:]
                upd[head, b] = new
                ending = jnp.exp(last) * ending + new
                decay = decay + last
            for owner in range(NZ):
                part[g, owning, owner, pl.ds(pl.multiple_of(i * 16, 16), 16), :] = ending[
                    owner * 16 : owner * 16 + 16
                ]
                part[g, owning, owner, pl.ds(PIECE + i, 1), :] = jnp.exp(decay)

        both_heads(one)

    later = lax.broadcasted_iota(jnp.int32, (SPAN, SPAN), 0) >= lax.broadcasted_iota(
        jnp.int32, (SPAN, SPAN), 1
    )

    def within(lo, hi):
        def turn(head, carry):
            for b in range(4):
                rows = pl.ds(b * SPAN, SPAN)
                scores = lax.dot_general(
                    q_ref[rows, lanes(head)],
                    k_ref[rows, lanes(head)],
                    LAST,
                    preferred_element_type=F32,
                )
                mine = col[head, rows, :]
                diff = jnp.concatenate([mine, mine], axis=1) - cum[pl.ds(head, 1), rows]
                weights = jnp.where(later, scores * jnp.exp(jnp.minimum(diff, 0.0)), 0.0)
                inner[head, rows, :] = jnp.dot(
                    weights.astype(BF16), v_ref[rows, lanes(head)], preferred_element_type=F32
                )
            return carry

        lax.fori_loop(lo, hi, turn, 0)

    def to_core(g):
        return keep(send(part.at[g, 1 - core], other.at[g], s_core.at[g], r_core.at[g], mate))

    def to_owners(g, copy):
        copy.wait_recv()

        def combine(owner, carry):
            mine, theirs_ = part[g, core, owner], other[g, owner]
            first = jnp.where(core == 0, mine, theirs_)
            second = jnp.where(core == 0, theirs_, mine)
            state, decay = join(first, second)
            chip[g, owner, :PIECE, :] = state
            chip[g, owner, PIECE:, :] = decay
            return carry

        lax.fori_loop(0, NZ, combine, 0)
        for i in range(1, NZ):
            to = lax.rem(z + i, NZ)
            send(chip.at[g, to], zin.at[g, z], s_z.at[g], r_z.at[g], at(y, to, core))
        keep(batch(chip.at[g, pl.ds(0, NZ - 1)], s_z.at[g]))
        zin[g, z] = chip[g, z]

    def to_rows(g):
        batch(zin.at[g, pl.ds(0, NZ - 1)], r_z.at[g]).wait_recv()
        state, decay = jnp.zeros((PIECE, D), F32), jnp.ones((8, D), F32)
        for j in range(NZ):
            pre[g, j, :PIECE, :] = state
            pre[g, j, PIECE:, :] = decay
            state, decay = join(jnp.concatenate([state, decay], axis=0), zin[g, j])
        yin[g, y, :PIECE, :] = state
        yin[g, y, PIECE:, :] = decay
        for i in range(1, NY):
            to = lax.rem(y + i, NY)
            send(yin.at[g, y], yin.at[g, y], s_y.at[g], r_y.at[g], at(to, z, core))
        keep(batch(yin.at[g, pl.ds(0, NY - 1)], s_y.at[g]))

    def to_chips(g):
        batch(yin.at[g, pl.ds(0, NY - 1)], r_y.at[g]).wait_recv()
        row = jnp.zeros((PIECE, D), F32)
        for j in range(NY):
            piece = yin[g, j]
            row = jnp.where(j < y, expand(piece) * row + piece[:PIECE], row)
        for j in range(NZ):
            piece = pre[g, j]
            back[g, j] = expand(piece) * row + piece[:PIECE]
        for i in range(1, NZ):
            to = lax.rem(z + i, NZ)
            send(back.at[g, to], chipin.at[g, z], s_zb.at[g], r_zb.at[g], at(y, to, core))
        keep(batch(back.at[g, pl.ds(0, NZ - 1)], s_zb.at[g]))
        chipin[g, z] = back[g, z]

    def to_cores(g):
        batch(chipin.at[g, pl.ds(0, NZ - 1)], r_zb.at[g]).wait_recv()

        def split(owner, carry):
            lead = jnp.where(core == 0, part[g, core, owner], other[g, owner])
            early = chipin[g, owner]
            late = expand(lead) * early + lead[:PIECE]
            give[g, owner] = jnp.where(core == 0, late, early)
            sin[g, core, owner] = jnp.where(core == 0, early, late)
            return carry

        lax.fori_loop(0, NZ, split, 0)
        return keep(send(give.at[g], sin.at[g, core], s_cb.at[g], r_cb.at[g], mate))

    def finish(g, owning):
        def one(i):
            head = 4 * g + 2 * owning + i
            state = jnp.concatenate(
                [
                    sin[g, owning, owner, pl.ds(pl.multiple_of(i * 16, 16), 16), :]
                    for owner in range(NZ)
                ],
                axis=0,
            )
            gain = gain_ref[pl.ds(head, 1), :]
            mean = jnp.zeros((1, D), F32)
            top = bottom = None
            for b in range(4):
                rows = pl.ds(b * SPAN, SPAN)
                high = state.astype(BF16)
                low = (state - high.astype(F32)).astype(BF16)
                both = jnp.dot(
                    q_ref[rows, lanes(head)],
                    jnp.concatenate([high, low], axis=1),
                    preferred_element_type=F32,
                )
                raw = inner[head, rows, :] + jnp.exp(col[head, rows, :]) * (both[:, :D] + both[:, D:])
                scale = jnp.sqrt(jnp.mean(raw * raw, axis=1, keepdims=True) + 1e-06)
                done = (raw / scale * gain).astype(BF16).astype(F32)
                mean = mean + jnp.sum(done, axis=0, keepdims=True)
                high_b = jnp.max(done, axis=0, keepdims=True)
                low_b = jnp.min(done, axis=0, keepdims=True)
                top = high_b if top is None else jnp.maximum(top, high_b)
                bottom = low_b if bottom is None else jnp.minimum(bottom, low_b)
                inner[head, rows, :] = done
                if b < 3:
                    last = col[head, pl.ds(b * SPAN + SPAN - 1, 1), :]
                    state = jnp.exp(last) * state + upd[head, b]
            mean = mean / (4 * SPAN)
            for b in range(4):
                rows = pl.ds(b * SPAN, SPAN)
                c_ref[rows, lanes(head)] = (inner[head, rows, :] - mean).astype(BF16)
            st_ref[pl.ds(head, 1), :] = mean
            st_ref[pl.ds(8 + head, 1), :] = top
            st_ref[pl.ds(16 + head, 1), :] = bottom

        both_heads(one)

    other_half = pl.ds(pl.multiple_of((1 - parity) * 512, 512), 512)
    half = pl.ds(pl.multiple_of(parity * 512, 512), 512)

    def columns(j):
        return pl.ds(pl.multiple_of(j * 256, 256), 256)

    def to_pair(j):
        return keep(
            send(
                c_ref.at[other_half, columns(j)],
                theirs.at[:, columns(j)],
                s_x.at[j],
                r_x.at[j],
                pair,
            )
        )

    def from_pair(j):
        arrived(
            c_ref.at[other_half, columns(j)], theirs.at[:, columns(j)], s_x.at[j], r_x.at[j], pair
        )

    targets = (far, north, south, y)

    def begin(seg):
        kind, first, wide = SEGMENTS[seg]
        cols = slice(first, first + wide)
        copies = []
        for i, target in enumerate(targets):
            rows = columns(target)
            if kind == DIAG:
                a, b = c_ref[:, rows], c_ref[:, cols]
            elif kind == CROSS:
                a, b = c_ref[half, rows], theirs[:, cols]
            else:
                a, b = theirs[:, rows], c_ref[half, cols]
            value = lax.dot_general(a, b, TOK, preferred_element_type=F32)
            grams[seg][i] = value.astype(BF16).reshape(NZ, 2, 16, wide)
            if i in (0, 3):
                span = pl.ds(0, 1) if i == 0 else pl.ds(1, 3)
                copies.append(
                    send(
                        grams[seg].at[span, :, 1 - core],
                        mates[seg].at[span],
                        s_c.at[seg],
                        r_c.at[seg, i // 3],
                        mate,
                    )
                )
        keep(batch(mates[seg], s_c.at[seg]))
        return copies

    def chip_sum(seg, i, which):
        return grams[seg][i, which, core].astype(F32) + mates[seg][i, which].astype(F32)

    def merge(a, b):
        return jnp.concatenate(
            [a[:8] + b[:8], jnp.maximum(a[8:16], b[8:16]), jnp.minimum(a[16:], b[16:])], axis=0
        )

    def add_mate(seg, copies):
        copies[0].wait_recv()

        def turn(i, carry):
            two = pl.ds(i * 2, 2)
            sums[seg][two] = chip_sum(seg, 0, two).astype(BF16)
            return carry

        lax.fori_loop(0, 4, turn, 0)
        edge = SEGMENTS[seg][2] // 2
        send(sums[seg].at[:, :, pl.ds(0, edge)], ylow[seg], s_y1.at[seg], r_y1.at[seg], at(north, z, core))
        send(sums[seg].at[:, :, pl.ds(edge, edge)], yhigh[seg], s_y1.at[seg], r_y1.at[seg], at(south, z, core))
        keep(batch(sums[seg], s_y1.at[seg]))
        return copies[1]

    def pass_on(seg, rest):
        batch(sums[seg], r_y1.at[seg]).wait_recv()
        rest.wait_recv()
        edge = SEGMENTS[seg][2] // 2

        def turn(i, carry):
            two = pl.ds(i * 2, 2)
            a = chip_sum(seg, 1, two)
            b = chip_sum(seg, 2, two)
            low = a[:, :, :edge] + ylow[seg][two].astype(F32)
            high = b[:, :, edge:] + yhigh[seg][two].astype(F32)
            ynext[seg][two, :, :edge] = low.astype(BF16)
            ynext[seg][two, :, edge:] = a[:, :, edge:].astype(BF16)
            yprev[seg][two, :, :edge] = b[:, :, :edge].astype(BF16)
            yprev[seg][two, :, edge:] = high.astype(BF16)
            return carry

        lax.fori_loop(0, 4, turn, 0)
        send(ynext[seg], yfirst[seg], s_y2.at[seg], r_y2.at[seg], at(north, z, core))
        send(yprev[seg], ylast[seg], s_y2.at[seg], r_y2.at[seg], at(south, z, core))
        keep(batch(mates[seg].at[pl.ds(0, 2)], s_y2.at[seg]))

    def to_z(seg):
        batch(mates[seg].at[pl.ds(0, 2)], r_y2.at[seg]).wait_recv()
        kind, first, wide = SEGMENTS[seg]
        tall = 1024 if kind == TURNED else 0
        start = first + (1024 if kind == CROSS else 0)
        spread = lax.dot_general(
            left[:, pl.ds(pl.multiple_of(tall + y * 256, 256), 256)],
            right[:, start : start + wide],
            TOK,
            preferred_element_type=F32,
        )
        spread = spread.reshape(NZ, 2, 16, wide) * (1024.0 if kind == DIAG else 512.0)
        spread = jnp.where(core == 0, spread[:, 0], spread[:, 1])
        got = chip_sum(seg, 3, pl.ds(0, NZ)) + yfirst[seg][...].astype(F32)
        got = got + ylast[seg][...].astype(F32) + spread
        zsend[seg][...] = got.astype(BF16)
        for i in range(0 if kind == TURNED else 1, NZ):
            to = lax.rem(z + i, NZ)
            peer = across(to) if kind == TURNED else at(y, to, core)
            send(zsend[seg].at[to], zgot[seg].at[z], s_zz.at[seg], r_zz.at[seg], peer)
        count = NZ if kind == TURNED else NZ - 1
        keep(batch(zsend[seg].at[pl.ds(0, count)], s_zz.at[seg]))
        if kind != TURNED:
            zgot[seg][z] = zsend[seg][z]

    def from_z(seg):
        count = NZ if SEGMENTS[seg][0] == TURNED else NZ - 1
        batch(zgot[seg].at[pl.ds(0, count)], r_zz.at[seg]).wait_recv()
        got = zgot[seg][0].astype(F32)
        for j in range(1, NZ):
            got = got + zgot[seg][j].astype(F32)
        return got

    def kv_ready(g):
        kv_in[g][0].wait()
        kv_in[g][1].wait()

    kv_ready(0)
    update(0, 1 - core)
    ready()
    b0 = to_core(0)
    update(0, core)
    columns_of(range(4, 8))
    kv_ready(1)
    update(1, 1 - core)
    b1 = to_core(1)
    to_owners(0, b0)
    update(1, core)
    to_owners(1, b1)
    q_in.wait()
    within(0, 6)
    to_rows(0)
    within(6, 7)
    to_rows(1)
    within(7, 8)
    to_chips(0)
    to_chips(1)
    e0 = to_cores(0)
    finish(0, core)
    to_pair(core)
    e0.wait_recv()
    finish(0, 1 - core)
    to_pair(1 - core)
    e1 = to_cores(1)
    finish(1, core)
    e1.wait_recv()
    finish(1, 1 - core)
    first = keep(send(st_ref, armate, s_s1, r_s1, mate))
    to_pair(2)
    to_pair(3)
    means[y, core] = st_ref[:8, :]

    def spread_rows(source, base):
        for j in range(8):
            piece = source[:, j, :]
            high = piece.astype(BF16)
            low = (piece - high.astype(F32)).astype(BF16)
            none = jnp.zeros_like(high)
            cols = slice(base + j * D, base + j * D + D)
            left[:, cols] = jnp.concatenate([high, high, low, none], axis=0)
            right[:, cols] = jnp.concatenate([high, low, high, none], axis=0)

    c0 = begin(0)
    first.wait_recv()
    means[y, 1 - core] = armate[:8, :]
    stz[z] = merge(st_ref[...], armate[...])
    for i in range(1, NZ):
        to = lax.rem(z + i, NZ)
        send(stz.at[z], stz.at[z], s_sz, r_sz, at(y, to, core))
    keep(batch(stz.at[pl.ds(0, NZ - 1)], s_sz))
    for i in range(1, NY):
        to = lax.rem(y + i, NY)
        send(means.at[y], means.at[y], s_g, r_g, at(to, z, core))
    keep(batch(means.at[pl.ds(0, NY - 1)], s_g))
    c1 = begin(1)
    p0 = add_mate(0, c0)
    p1 = add_mate(1, c1)
    pass_on(0, p0)
    from_pair(core)
    from_pair(1 - core)
    c2 = begin(2)
    pass_on(1, p1)
    batch(stz.at[pl.ds(0, NZ - 1)], r_sz).wait_recv()
    sty[y] = functools.reduce(merge, [stz[j] for j in range(NZ)])
    for i in range(1, NY):
        to = lax.rem(y + i, NY)
        send(sty.at[y], sty.at[y], s_sy, r_sy, at(to, z, core))
    keep(batch(sty.at[pl.ds(0, NY - 1)], s_sy))
    p2 = add_mate(2, c2)
    from_pair(2)
    c3 = begin(3)
    batch(means.at[pl.ds(0, NY - 1)], r_g).wait_recv()
    batch(sty.at[pl.ds(0, NY - 1)], r_sy).wait_recv()
    every = functools.reduce(merge, [sty[j] for j in range(NY)])
    shift_ref[...] = (every[8:16] + every[16:]) / 2.0
    writes = [load(shift_ref, shift_hbm, s_out.at[0])]
    off[...] = means[...].reshape(NY * 2, 8, D) - (every[:8] / 64.0)[None]
    offset = keep(send(off, offin, s_m, r_m, pair))
    spread_rows(off, 0)
    to_z(0)
    to_z(1)
    pass_on(2, p2)
    p3 = add_mate(3, c3)
    from_pair(3)
    c4 = begin(4)
    c5 = begin(5)
    p4 = add_mate(4, c4)
    p5 = add_mate(5, c5)
    pass_on(3, p3)
    c6 = begin(6)
    p6 = add_mate(6, c6)
    offset.wait_recv()
    spread_rows(offin, 1024)
    to_z(2)
    pass_on(4, p4)
    pass_on(5, p5)
    to_z(3)
    pass_on(6, p6)
    diag_ref[...] = jnp.concatenate([from_z(0), from_z(1)], axis=1) / 65536.0
    block = pl.ds(pl.multiple_of(parity * 1024, 1024), 1024)
    writes.append(load(diag_ref, cov_hbm.at[:, block], s_out.at[1]))
    to_z(4)
    to_z(5)
    to_z(6)
    cross_ref[:, :512] = from_z(2)
    cross_ref[:, 512:768] = from_z(3)
    cross_ref[:, :512] = (cross_ref[:, :512] + from_z(4)) / 65536.0
    turned1 = from_z(5)
    cross_ref[:, 512:768] = (cross_ref[:, 512:768] + turned1[:, :256]) / 65536.0
    cross_ref[:, 768:] = (from_z(6) + turned1[:, 256:]) / 65536.0
    block = pl.ds(pl.multiple_of((1 - parity) * 1024, 1024), 1024)
    writes.append(load(cross_ref, cov_hbm.at[:, block], s_out.at[2]))
    for copy in writes:
        copy.wait()
    for copy in out:
        copy.wait_send()


def whole(q, k, v, log_decay, gain):
    count, width = q.shape
    vm = pl.BlockSpec(memory_space=pltpu.VMEM)
    hbm = pl.BlockSpec(memory_space=pl.ANY)
    dma = pltpu.SemaphoreType.DMA

    def f32(*shape):
        return pltpu.VMEM(shape, F32)

    def bf16(*shape):
        return pltpu.VMEM(shape, BF16)

    def per_segment(*shape, share=1):
        return tuple(pltpu.VMEM((*shape, wide // share), BF16) for _, _, wide in SEGMENTS)

    return pl.pallas_call(
        kernel,
        out_shape=(
            jax.ShapeDtypeStruct((8, D), F32),
            jax.ShapeDtypeStruct((16, 2048), F32),
        ),
        in_specs=[hbm, hbm, hbm, vm, vm],
        out_specs=(hbm, hbm),
        scratch_shapes=[
            bf16(count, width),
            bf16(count, width),
            bf16(count, width),
            bf16(count, width),
            f32(24, D),
            f32(8, 1024),
            f32(8, 1024, D),
            f32(8, 1024, D),
            f32(8, 4, D, D),
            f32(2, 2, NZ, PIECE + 8, D),
            f32(2, NZ, PIECE + 8, D),
            f32(2, NZ, PIECE + 8, D),
            f32(2, NZ, PIECE + 8, D),
            f32(2, NZ, PIECE + 8, D),
            f32(2, NY, PIECE + 8, D),
            f32(2, NZ, PIECE, D),
            f32(2, NZ, PIECE, D),
            f32(2, NZ, PIECE, D),
            f32(2, 2, NZ, PIECE, D),
            bf16(512, 1024),
            f32(8, D),
            f32(16, 1024),
            f32(16, 1024),
            f32(NY, 2, 8, D),
            f32(24, D),
            f32(NZ, 24, D),
            f32(NY, 24, D),
            f32(2 * NY, 8, D),
            f32(2 * NY, 8, D),
            bf16(32, 2048),
            bf16(32, 2048),
            per_segment(NY, NZ, 2, 16),
            per_segment(NY, NZ, 16),
            per_segment(NZ, 16),
            per_segment(NZ, 16, share=2),
            per_segment(NZ, 16, share=2),
            per_segment(NZ, 16),
            per_segment(NZ, 16),
            per_segment(NZ, 16),
            per_segment(NZ, 16),
            per_segment(NZ, 16),
            per_segment(NZ, 16),
            dma((5,)), dma((2,)), dma((2,)), dma((2,)), dma((2,)), dma((2,)), dma((2,)),
            dma((2,)), dma((2,)), dma((2,)), dma((2,)),
            dma, dma, dma((4,)), dma((4,)), dma((SEGS,)), dma((SEGS, 2)),
            dma((SEGS,)), dma((SEGS,)), dma((SEGS,)), dma((SEGS,)), dma((SEGS,)), dma((SEGS,)), dma((3,)),
            dma, dma, dma, dma, dma, dma, dma, dma,
        ],
        compiler_params=pltpu.CompilerParams(
            collective_id=0, has_side_effects=True, vmem_limit_bytes=60 * 1024 * 1024
        ),
        name="whole",
    )(q, k, v, log_decay, gain.reshape(8, D))


def hand_kernel(a_ref, b_ref, c_ref, d_ref):
    c_ref[...] = a_ref[...]
    d_ref[...] = b_ref[...]


def hand_out(shift, covariance):
    vm = pl.BlockSpec(memory_space=pltpu.VMEM)
    return pl.pallas_call(
        hand_kernel,
        out_shape=(
            jax.ShapeDtypeStruct(shift.shape, F32),
            jax.ShapeDtypeStruct(covariance.shape, F32),
        ),
        in_specs=[vm] * 2,
        out_specs=(vm, vm),
        name="hand_out",
    )(shift, covariance)


def body(queries, keys, values, log_decay, gain):
    shift, covariance = hand_out(*whole(queries, keys, values, log_decay, gain))
    return (shift.reshape(-1), covariance)


def solution(mesh):
    placed = (P("ctx", "head"), P("ctx", "head"), P("ctx", "head"), P("head", "ctx"), P("head"))
    return jax.shard_map(
        body,
        mesh=mesh,
        in_specs=placed,
        out_specs=(P("head"), P(("head", "ctx"), None)),
        check_vma=False,
    )
```
